256 devices in a mesh: row: 32 (over y, z), col: 8 (over x, core).
Axes of the slice: x: 4, y: 4, z: 8, core: 2. Of those that a mesh axis runs over, the one named last changes fastest.
Arguments:
- panel_one: bfloat16 [512, 32768], P('col', 'row'), may hold values from -1.1953125 to 1.1953125
- panel_two: bfloat16 [512, 32768], P('col', 'row'), may hold values from -3 to 3
- inverse_one: bfloat16 [512, 512], replicated
- inverse_two: bfloat16 [512, 512], replicated
- column_blocks: int32 [4], replicated, may hold values from 0 to 255, as said below
- row_map: int32 [256], P('row'), may hold values from 0 to 255, as said below
- targets: bfloat16 [32, 8, 128, 128, 128], P('row', 'col'), may hold values from -6 to 6
- rows_one: int32 [32, 8, 128], P('row', 'col'), may hold values from 0 to 255, as said below
- cols_one: int32 [32, 8, 128], P('row', 'col'), may hold values from 0 to 255, as said below
- rows_two: int32 [32, 8, 128], P('row', 'col'), may hold values from 0 to 255, as said below
- cols_two: int32 [32, 8, 128], P('row', 'col'), may hold values from 0 to 255, as said below
Outputs:
- lower_one: bfloat16 [512, 32768], P('col', 'row')
- lower_two: bfloat16 [512, 32768], P('col', 'row')
- trailing: bfloat16 [32, 8, 128, 128, 128], P('row', 'col')
The draws below stay inside these ranges and needn't reach their ends.
Inputs may be any that keep to these rules, and one draw needn't show every extreme that they name: `column_blocks`: the entries are distinct. row_map[j] // 8 equals j // 8; within each aligned run of 8 entries every value of the run appears once. rows_one[r, c, s] // 8 equals r. cols_one[r, c, s] % 8 equals c. rows_two[r, c, s] // 8 equals r. cols_two[r, c, s] % 8 equals c.
All inputs are finite; a program needn't handle non-finite values.
Results may differ from the reference program's by a relative error of at most 0.006.
Values may be sent and summed in bfloat16 or wider, within the bound.
A program may use at most 192 MiB of HBM per device.

```python
import math
import jax
import jax.numpy as jnp
from jax import lax

W = 512
B = 128
RB_DEV = 8
TB_DEV = 128
GR = 32
GC = 8
ROWBLOCKS = 256
ROWS = 32768
NCB = 4


def triangle(key, diag_low, diag_high, off_scale):
    key_diag, key_off = jax.random.split(key)
    positions = jnp.arange(W)
    lower_mask = positions[:, None] > positions[None, :]
    diagonal = jax.random.uniform(key_diag, (W,), jnp.float32, diag_low, diag_high)
    spread = jax.random.normal(key_off, (W, W), jnp.float32) * (off_scale / math.sqrt(W))
    matrix = jnp.where(lower_mask, spread, 0.0) + jnp.diag(diagonal)
    return matrix.astype(jnp.bfloat16)


def draw_inverse_one(key, part):
    return triangle(jax.random.fold_in(key, 11), 0.6, 1.0, 0.4)


def draw_inverse_two(key, part):
    return triangle(jax.random.fold_in(key, 12), 0.15, 0.3, 0.08)


def draw_column_blocks(key, part):
    return jax.random.permutation(key, ROWBLOCKS)[:NCB].astype(jnp.int32)


def draw_row_map(key, part):
    scores = jax.random.randint(key, (GR, RB_DEV), 0, 1 << 20, dtype=jnp.int32) * RB_DEV
    scores = scores + jnp.arange(RB_DEV, dtype=jnp.int32)[None, :]
    order = jnp.argsort(scores, axis=1, stable=True).astype(jnp.int32)
    base_rows = jnp.arange(GR, dtype=jnp.int32)[:, None] * RB_DEV
    return (base_rows + order).reshape(ROWBLOCKS).astype(jnp.int32)


def owner_rows(key):
    grid_rows = jnp.arange(GR, dtype=jnp.int32).reshape(GR, 1, 1)
    offsets = jax.random.randint(key, (GR, GC, TB_DEV), 0, RB_DEV, dtype=jnp.int32)
    return (grid_rows * RB_DEV + offsets).astype(jnp.int32)


def owner_cols(key):
    grid_cols = jnp.arange(GC, dtype=jnp.int32).reshape(1, GC, 1)
    strides = jax.random.randint(key, (GR, GC, TB_DEV), 0, ROWBLOCKS // GC, dtype=jnp.int32)
    return (grid_cols + GC * strides).astype(jnp.int32)


def draw_rows_one(key, part):
    return owner_rows(jax.random.fold_in(key, 21))


def draw_cols_one(key, part):
    return owner_cols(jax.random.fold_in(key, 22))


def draw_rows_two(key, part):
    return owner_rows(jax.random.fold_in(key, 23))


def draw_cols_two(key, part):
    return owner_cols(jax.random.fold_in(key, 24))


def shard_levels(own_key, shape, cuts, smallest, high):
    def one(dim, shards_of):
        steps = jax.random.uniform(jax.random.fold_in(jax.random.fold_in(own_key, 6), dim), (shards_of,), jnp.float32, smallest / len(cuts), high / len(cuts))
        return jnp.repeat(jnp.exp(steps), shape[dim] // shards_of).reshape((-1,) + (1,) * (len(shape) - dim - 1))

    loudness = one(*cuts[0])
    for cut in cuts[1:]:
        loudness = loudness * one(*cut)
    return loudness


def normal_values(rng, extent, width, most, pieces=(), kind=jnp.bfloat16):
    entries = width * jax.random.normal(rng, extent, jnp.float32)
    if pieces:
        entries = entries * shard_levels(rng, extent, pieces, -0.22, 0.18)
    return jnp.clip(entries, -most, most).astype(kind)


def setup_inputs(seed: int = 0) -> dict:
    key_list = jax.random.split(jax.random.key(seed), 12)
    panel_one = normal_values(key_list[0], (W, ROWS), 0.2, 1.1953125, ((0, 8), (1, 32)))
    panel_two = normal_values(key_list[1], (W, ROWS), 0.5, 3.0, ((0, 8), (1, 32)))
    inverse_one = draw_inverse_one(jax.random.fold_in(key_list[11], 71), 0)
    inverse_two = draw_inverse_two(jax.random.fold_in(key_list[11], 71), 0)
    column_blocks = draw_column_blocks(jax.random.fold_in(key_list[11], 71), 0)
    row_map = draw_row_map(jax.random.fold_in(key_list[11], 71), 0)
    targets = normal_values(key_list[6], (GR, GC, TB_DEV, B, B), 1.0, 6.0, ((0, 32), (1, 8)))
    rows_one = draw_rows_one(jax.random.fold_in(key_list[11], 71), 0)
    cols_one = draw_cols_one(jax.random.fold_in(key_list[11], 71), 0)
    rows_two = draw_rows_two(jax.random.fold_in(key_list[11], 71), 0)
    cols_two = draw_cols_two(jax.random.fold_in(key_list[11], 71), 0)
    return dict(panel_one=panel_one, panel_two=panel_two, inverse_one=inverse_one, inverse_two=inverse_two, column_blocks=column_blocks, row_map=row_map, targets=targets, rows_one=rows_one, cols_one=cols_one, rows_two=rows_two, cols_two=cols_two)


def reference(panel_one, panel_two, inverse_one, inverse_two, column_blocks, row_map, targets, rows_one, cols_one, rows_two, cols_two):
    lower_one = jnp.dot(inverse_one, panel_one, preferred_element_type=jnp.float32).astype(jnp.bfloat16)
    blocks_one = lower_one.reshape(W, ROWBLOCKS, B)
    bridge = jnp.take(blocks_one, column_blocks.astype(jnp.int32), axis=1).reshape(W, W)
    mapped = jnp.take(blocks_one, row_map.astype(jnp.int32), axis=1).reshape(W, ROWS)
    update = jnp.dot(bridge.T, mapped, preferred_element_type=jnp.float32)
    updated = (panel_two.astype(jnp.float32) - update).astype(jnp.bfloat16)
    lower_two = jnp.dot(inverse_two, updated, preferred_element_type=jnp.float32).astype(jnp.bfloat16)
    blocks_two = lower_two.reshape(W, ROWBLOCKS, B)

    def slot_update(slot_pack):
        first_rows, first_cols, second_rows, second_cols, old_blocks = slot_pack
        left_one = jnp.take(blocks_one, first_rows, axis=1).astype(jnp.float32)
        right_one = jnp.take(blocks_one, first_cols, axis=1).astype(jnp.float32)
        left_two = jnp.take(blocks_two, second_rows, axis=1).astype(jnp.float32)
        right_two = jnp.take(blocks_two, second_cols, axis=1).astype(jnp.float32)
        term_one = jnp.einsum("wsx,wsy->sxy", left_one, right_one)
        term_two = jnp.einsum("wsx,wsy->sxy", left_two, right_two)
        return (old_blocks.astype(jnp.float32) - term_one - term_two).astype(jnp.bfloat16)

    grid_count = GR * GC
    trailing = lax.map(slot_update, (rows_one.reshape(grid_count, TB_DEV).astype(jnp.int32),
                                      cols_one.reshape(grid_count, TB_DEV).astype(jnp.int32),
                                      rows_two.reshape(grid_count, TB_DEV).astype(jnp.int32),
                                      cols_two.reshape(grid_count, TB_DEV).astype(jnp.int32),
                                      targets.reshape(grid_count, TB_DEV, B, B)))
    return lower_one, lower_two, trailing.reshape(GR, GC, TB_DEV, B, B)
```

```python
import functools
import heapq

import jax
import jax.numpy as jnp
from jax import lax
from jax.experimental import pallas as pl
from jax.experimental.pallas import tpu as pltpu
from jax.sharding import PartitionSpec as P

MESH = pl.DeviceIdType.MESH
NY, NZ, NX, NC = 4, 8, 4, 2

PART_A, HALF_A0, HALF_A1 = (0, 304), (0, 160), (160, 144)
PART_B, HALF_B0, HALF_B1 = (304, 208), (304, 112), (416, 96)
STEP = {"y+": (1, 0), "y-": (-1, 0), "z+": (0, 1), "z-": (0, -1)}
OWN_SENDS = (
    ("z+", PART_A),
    ("z-", PART_A),
    ("y+", PART_B),
    ("y-", PART_B),
    ("y+", PART_A),
    ("y-", PART_A),
    ("z+", PART_B),
    ("z-", PART_B),
)


def wrapped(value, size):
    value %= size
    return value - size if value > size // 2 else value


def next_source(source, way):
    dy, dz = STEP[way]
    return (wrapped(source[0] - dy, NY), wrapped(source[1] - dz, NZ))


def forwards(way, piece, source, seen):
    sy, sz = source
    if piece[0] < PART_A[1]:
        first, second = HALF_A0, HALF_A1
        if way[0] == "z":
            half = first if way == "z+" else second
            out = [(way, PART_A)] if abs(sz) < 3 else []
            if abs(sz) == 3:
                out.append((way, half))
            if abs(sz) < 4 or {first, second} <= seen:
                out += [("y+", PART_A), ("y-", PART_A)]
            return out
        return [(way, first if way == "y+" else second)] if abs(sy) == 1 else []
    first, second = HALF_B0, HALF_B1
    if way[0] == "y":
        out = []
        if abs(sy) == 1:
            out.append((way, first if way == "y+" else second))
        if abs(sy) == 1 or {first, second} <= seen:
            out += [("z+", PART_B), ("z-", PART_B)]
        return out
    if abs(sz) < 3:
        return [(way, PART_B)]
    return [(way, first if way == "z+" else second)] if abs(sz) == 3 else []


def gather_plan(rate=47.0, latency=1.7):
    free = dict.fromkeys(STEP, 0.0)
    seen, heap, plan = {}, [], []

    def send(now, way, piece, source):
        free[way] = max(now, free[way]) + piece[1] * 256 / 1000 / rate
        heapq.heappush(
            heap, (free[way] + latency, len(heap) + len(plan), way, piece, next_source(source, way))
        )

    for way, piece in OWN_SENDS:
        send(0.0, way, piece, (0, 0))
    while heap:
        now, _, way, piece, source = heapq.heappop(heap)
        seen.setdefault(source, set()).add(piece)
        out = forwards(way, piece, source, seen[source])
        plan.append((now, way, piece, source, out))
        for onward, part in out:
            send(now, onward, part, source)
    return plan


PLAN = gather_plan()
EVENT = {(way, piece, source): i for i, (_, way, piece, source, _) in enumerate(PLAN)}
N_EVENTS = len(PLAN)


def tile_order():
    rows, done = {}, []
    for now, _, piece, source, _ in PLAN:
        rows[source] = rows.get(source, 0) + piece[1]
        if rows[source] == 512:
            done.append((now, source))
    return [(0.0, (0, 0))] + done


def kernel(
    panel_one,
    panel_two,
    inverse_one,
    inverse_two,
    targets,
    column_blocks,
    row_map,
    rows_one,
    cols_one,
    rows_two,
    cols_two,
    lower_one,
    lower_two,
    trailing,
    slab_one,
    slab_two,
    full_one,
    full_two,
    inv_one,
    inv_two,
    own_raw,
    pick,
    ring_z,
    mid,
    ring_y,
    raw_bridge,
    bridge_t,
    blocks_one,
    blocks_two,
    left_one,
    left_two,
    tiles,
    products,
    partial,
    staged,
    local_sem,
    out_sem,
    x_send,
    x_recv,
    side_recv,
    swap_send,
    swap_recv,
    sum_send,
    sum_recv,
    tile_send,
    tile_recv,
):
    f32, bf16 = jnp.float32, jnp.bfloat16
    row, col = lax.axis_index("row"), lax.axis_index("col")
    y, z = row // NZ, row % NZ
    x, core = col // NC, col % NC
    slab = slab_one.shape[1]
    base = pl.multiple_of(col * slab, slab)

    def row_at(dy, dz):
        return ((y + dy + NY) % NY) * NZ + (z + dz + NZ) % NZ

    def col_at(dx):
        return ((x + dx) % NX) * NC + core

    partner = x * NC + (1 - core)

    def remote(src, dst, send, recv, device):
        return pltpu.make_async_remote_copy(
            src_ref=src, dst_ref=dst, send_sem=send, recv_sem=recv, device_id=device, device_id_type=MESH
        )

    def await_recv(ref, sem):
        remote(ref, ref, tile_send.at[0], sem, (row, partner)).wait_recv()

    def await_send(ref, sem):
        remote(ref, ref, sem, tile_recv.at[0, 0], (row, partner)).wait_send()

    loads = []
    n_blocks = slab_one.shape[0]
    for which, (panel, mine) in enumerate(((panel_one, slab_one), (panel_two, slab_two))):
        for j in range(n_blocks):
            loads.append(pltpu.make_async_copy(panel.at[:, pl.ds(j * 128, 128)], mine.at[j], local_sem.at[which]))
    for copy in loads:
        copy.start()
    load_inv_one = pltpu.make_async_copy(inverse_one, inv_one, local_sem.at[2])
    load_inv_two = pltpu.make_async_copy(inverse_two, inv_two, local_sem.at[3])
    load_targets = pltpu.make_async_copy(targets, staged, local_sem.at[4])
    load_inv_one.start()
    load_inv_two.start()
    load_targets.start()

    barrier = pltpu.get_barrier_semaphore()
    in_row = [(row, (col + d) % (NX * NC)) for d in range(1, NX * NC)]
    along_z = [(row_at(0, d), col) for d in range(1, NZ)]
    along_y = [(row_at(d, 0), col) for d in range(1, NY)]
    for device in in_row + along_z + along_y:
        pl.semaphore_signal(barrier, inc=1, device_id=device, device_id_type=MESH)
    pltpu.make_async_copy(slab_one, slab_one, local_sem.at[0]).wait()
    pltpu.make_async_copy(slab_two, slab_two, local_sem.at[1]).wait()
    keep_one = pltpu.make_async_copy(slab_one, full_one.at[:, pl.ds(base, slab), :], local_sem.at[5])
    keep_two = pltpu.make_async_copy(slab_two, full_two.at[:, pl.ds(base, slab), :], local_sem.at[6])
    keep_raw = pltpu.make_async_copy(slab_one.at[col], own_raw.at[pl.ds(base, slab), :], local_sem.at[7])
    keep_one.start()
    keep_two.start()
    keep_raw.start()
    pl.semaphore_wait(barrier, len(in_row) + len(along_z) + len(along_y))

    for _, peer in in_row:
        remote(
            slab_one.at[peer], own_raw.at[pl.ds(base, slab), :], swap_send, swap_recv, (row, peer)
        ).start()

    for k in range(4):
        chosen = column_blocks[k]
        block = slab_one[chosen % n_blocks]
        block = jnp.where(chosen // n_blocks == row, block.astype(f32), 0.0).astype(bf16)
        pick[2 * k] = block[:32]
        pick[2 * k + 1] = block[32:]

    def spread(mine, full, which):
        for dx in range(1, NX):
            remote(
                mine, full.at[:, pl.ds(base, slab), :], x_send.at[which], x_recv.at[which, dx - 1], (row, col_at(dx))
            ).start()
        remote(
            mine, full.at[:, pl.ds(base, slab), :], x_send.at[which], side_recv.at[which], (row, partner)
        ).start()

    def pass_on(full, which, dx):
        ref = full.at[:, pl.ds(pl.multiple_of(col_at(NX - dx) * slab, slab), slab), :]
        await_recv(ref, x_recv.at[which, dx - 1])
        remote(ref, ref, x_send.at[which], side_recv.at[which], (row, partner)).start()

    def side_wait(full, which):
        await_recv(full.at[:, pl.ds(0, NX * slab), :], side_recv.at[which])

    def sum_z_send():
        for d in range(1, NZ):
            remote(
                pick.at[(z + d) % NZ], ring_z.at[d - 1], sum_send.at[0], sum_recv.at[0], (row_at(0, d), col)
            ).start()

    piece_k = z // 2
    piece_rows = pl.ds(pl.multiple_of(base + 32 * (z % 2), 32), 32)

    def sum_y_send():
        await_recv(ring_z, sum_recv.at[0])
        total = pick[z].astype(f32)
        for d in range(NZ - 1):
            total += ring_z[d].astype(f32)
        mid[...] = total.astype(bf16)
        for d in range(1, NY):
            remote(mid, ring_y.at[d - 1], sum_send.at[1], sum_recv.at[1], (row_at(d, 0), col)).start()

    def sum_z_return():
        await_recv(ring_y, sum_recv.at[1])
        total = mid[...].astype(f32)
        for d in range(NY - 1):
            total += ring_y[d].astype(f32)
        raw_bridge[piece_k, piece_rows, :] = total.astype(bf16)
        ref = raw_bridge.at[piece_k, piece_rows, :]
        for d in range(1, NZ):
            remote(ref, ref, sum_send.at[2], sum_recv.at[2], (row_at(0, d), col)).start()

    def bridge_spread():
        await_recv(ring_z, sum_recv.at[2])
        spread(raw_bridge.at[:, pl.ds(base, slab), :], raw_bridge, 2)

    def tile_copy(p, way, piece, source):
        ref = tiles.at[p, row_at(*source), pl.ds(*piece), :]
        event = EVENT[(way, piece, next_source(source, way))]
        remote(ref, ref, tile_send.at[p], tile_recv.at[p, event], (row_at(*STEP[way]), col)).start()

    def own_sends(p):
        for way, piece in OWN_SENDS:
            tile_copy(p, way, piece, (0, 0))

    def tile_event(p, index):
        _, _, piece, source, out = PLAN[index]
        await_recv(tiles.at[p, row_at(*source), pl.ds(*piece), :], tile_recv.at[p, index])
        for way, part in out:
            tile_copy(p, way, part, source)

    def dot(a, b):
        return jnp.dot(a, b, preferred_element_type=f32)

    def first_block():
        await_recv(own_raw.at[pl.ds(0, (NX * NC - 1) * slab), :], swap_recv)
        tiles[0, row] = dot(inv_one[...], own_raw[...]).astype(bf16)

    def store_pair(blocks, left, i, value):
        for h in range(2):
            part = value[:, h * 128 : (h + 1) * 128]
            blocks[2 * i + h] = part.astype(bf16)
            left[pl.ds(pl.multiple_of((2 * i + h) * 128, 128), 128), :] = part.T.astype(bf16)

    def factor_one():
        @pl.loop(0, n_blocks // 2)
        def _(i):
            pair = jnp.concatenate([full_one[2 * i], full_one[2 * i + 1]], axis=1)
            store_pair(blocks_one, left_one, i, dot(inv_one[...], pair))

    def bridge_build():
        @pl.loop(0, 4)
        def _(k):
            value = dot(inv_one[...], raw_bridge[k])
            bridge_t[pl.ds(pl.multiple_of(k * 128, 128), 128), :] = value.T.astype(bf16)

    def pair_two(i):
        mapped = jnp.concatenate(
            [blocks_one[row_map[2 * i] % n_blocks], blocks_one[row_map[2 * i + 1] % n_blocks]], axis=1
        )
        pair = jnp.concatenate([full_two[2 * i], full_two[2 * i + 1]], axis=1)
        updated = (pair.astype(f32) - dot(bridge_t[...], mapped)).astype(bf16)
        store_pair(blocks_two, left_two, i, dot(inv_two[...], updated))

    def factor_two_own():
        pair_two(col // 2)
        tiles[1, row] = blocks_two[col]

    def factor_two_rest():
        @pl.loop(1, n_blocks // 2)
        def _(i):
            pair_two((col // 2 + i) % (n_blocks // 2))

    def products_of(p, left, first, second):
        t0, t1 = row_at(*first), row_at(*second)

        @pl.loop(0, 2)
        def _(m):
            pair = jnp.concatenate([tiles[p, t0], tiles[p, t1]], axis=1)
            value = dot(left[pl.ds(pl.multiple_of(m * 512, 512), 512), :], pair)
            for h, t in enumerate((t0, t1)):
                products[pl.ds(t * n_blocks + 4 * m, 4)] = value[:, h * 128 : (h + 1) * 128].reshape(4, 128, 128)

    n_slots = staged.shape[0]

    def combine_one():
        load_targets.wait()

        @pl.loop(0, n_slots)
        def _(s):
            index = (cols_one[s] // n_blocks) * n_blocks + rows_one[s] % n_blocks
            partial[s] = staged[s].astype(f32) - products[index]

    group = 16

    def result_copy(g):
        return pltpu.make_async_copy(
            staged.at[pl.ds(g * group, group)], trailing.at[pl.ds(g * group, group)], out_sem.at[g]
        )

    def combine_two():
        for g in range(n_slots // group):

            @pl.loop(g * group, (g + 1) * group)
            def _(s):
                index = (cols_two[s] // n_blocks) * n_blocks + rows_two[s] % n_blocks
                staged[s] = (partial[s] - products[index]).astype(bf16)

            result_copy(g).start()

    def write_lower(blocks, out, which):
        return [
            pltpu.make_async_copy(
                blocks.at[j, pl.ds(base, slab), :], out.at[:, pl.ds(j * 128, 128)], local_sem.at[8 + which]
            )
            for j in range(n_blocks)
        ]

    def start_all(copies):
        for copy in copies:
            copy.start()

    lower_copies = write_lower(blocks_one, lower_one, 0) + write_lower(blocks_two, lower_two, 1)

    sum_z_send()
    spread(slab_one, full_one, 0)
    spread(slab_two, full_two, 1)
    load_inv_one.wait()
    load_inv_two.wait()
    keep_raw.wait()
    keep_one.wait()
    keep_two.wait()
    first_block()
    own_sends(0)

    one, two = 0.0, 18.5
    work = [
        (0.6, sum_y_send),
        (3.6, sum_z_return),
        (4.0, lambda: pass_on(full_one, 0, 1)),
        (4.1, lambda: pass_on(full_one, 0, 3)),
        (4.9, lambda: pass_on(full_one, 0, 2)),
        (6.5, lambda: side_wait(full_one, 0)),
        (6.6, factor_one),
        (6.7, lambda: start_all(lower_copies[:n_blocks])),
        (8.6, bridge_spread),
        (9.0, lambda: pass_on(full_two, 1, 1)),
        (9.1, lambda: pass_on(full_two, 1, 3)),
        (10.6, lambda: pass_on(full_two, 1, 2)),
        (12.2, lambda: side_wait(full_two, 1)),
        (13.8, lambda: pass_on(raw_bridge, 2, 1)),
        (13.9, lambda: pass_on(raw_bridge, 2, 3)),
        (14.8, lambda: pass_on(raw_bridge, 2, 2)),
        (16.3, lambda: side_wait(raw_bridge, 2)),
        (16.4, bridge_build),
        (16.5, factor_two_own),
        (16.6, lambda: own_sends(1)),
        (16.7, factor_two_rest),
        (16.8, lambda: start_all(lower_copies[n_blocks:])),
    ]
    for i, (now, *_) in enumerate(PLAN):
        work.append((one + now, functools.partial(tile_event, 0, i)))
        work.append((two + now, functools.partial(tile_event, 1, i)))
    order = tile_order()
    for i in range(0, len(order), 2):
        now, pair = order[i + 1][0], (order[i][1], order[i + 1][1])
        work.append((max(one + now, 6.61) + 0.01, functools.partial(products_of, 0, left_one, *pair)))
        work.append((max(two + now, one + PLAN[-1][0] + 0.1) + 0.01, functools.partial(products_of, 1, left_two, *pair)))
    work.append((one + PLAN[-1][0] + 0.1, combine_one))
    for _, step in sorted(work, key=lambda item: item[0]):
        step()
    combine_two()

    for g in range(n_slots // group):
        result_copy(g).wait()
    pltpu.make_async_copy(lower_one, lower_one, local_sem.at[8]).wait()
    pltpu.make_async_copy(lower_two, lower_two, local_sem.at[9]).wait()
    await_send(own_raw.at[pl.ds(0, (NX * NC - 1) * slab), :], swap_send)
    await_send(ring_z, sum_send.at[0])
    await_send(ring_y, sum_send.at[1])
    await_send(ring_z, sum_send.at[2])
    await_send(full_one.at[pl.ds(0, n_blocks - 1)], x_send.at[0])
    await_send(full_two.at[pl.ds(0, n_blocks - 1)], x_send.at[1])
    await_send(full_two.at[pl.ds(0, n_blocks - 1), pl.ds(0, 256), :], x_send.at[2])
    await_send(tiles.at[0, pl.ds(0, NY * NZ - 1)], tile_send.at[0])
    await_send(tiles.at[1, pl.ds(0, NY * NZ - 1)], tile_send.at[1])


def per_device(
    panel_one,
    panel_two,
    inverse_one,
    inverse_two,
    column_blocks,
    row_map,
    targets,
    rows_one,
    cols_one,
    rows_two,
    cols_two,
):
    slab, row_count = panel_one.shape
    width = inverse_one.shape[0]
    size = targets.shape[-1]
    n_slots = targets.shape[2]
    n_blocks = row_count // size
    n_rows = NY * NZ
    bf16, f32 = jnp.bfloat16, jnp.float32
    vmem = pltpu.VMEM
    dma = pltpu.SemaphoreType.DMA
    in_hbm = pl.BlockSpec(memory_space=pl.ANY)
    in_smem = pl.BlockSpec(memory_space=pltpu.SMEM)
    lower_one, lower_two, trailing = pl.pallas_call(
        kernel,
        out_shape=(
            jax.ShapeDtypeStruct(panel_one.shape, bf16),
            jax.ShapeDtypeStruct(panel_two.shape, bf16),
            jax.ShapeDtypeStruct((n_slots, size, size), bf16),
        ),
        in_specs=[in_hbm] * 5 + [in_smem] * 6,
        out_specs=(in_hbm,) * 3,
        scratch_shapes=[
            vmem((n_blocks, slab, size), bf16),
            vmem((n_blocks, slab, size), bf16),
            vmem((n_blocks, width, size), bf16),
            vmem((n_blocks, width, size), bf16),
            vmem((width, width), bf16),
            vmem((width, width), bf16),
            vmem((width, size), bf16),
            vmem((8, 32, size), bf16),
            vmem((NZ - 1, 32, size), bf16),
            vmem((32, size), bf16),
            vmem((NY - 1, 32, size), bf16),
            vmem((4, width, size), bf16),
            vmem((width, width), bf16),
            vmem((n_blocks, width, size), bf16),
            vmem((n_blocks, width, size), bf16),
            vmem((row_count, width), bf16),
            vmem((row_count, width), bf16),
            vmem((2, n_rows, width, size), bf16),
            vmem((n_rows * n_blocks, size, size), f32),
            vmem((n_slots, size, size), f32),
            vmem((n_slots, size, size), bf16),
            dma((10,)),
            dma((8,)),
            dma((3,)),
            dma((3, NX - 1)),
            dma((3,)),
            dma,
            dma,
            dma((3,)),
            dma((3,)),
            dma((2,)),
            dma((2, N_EVENTS)),
        ],
        compiler_params=pltpu.CompilerParams(
            collective_id=0, has_side_effects=True, vmem_limit_bytes=62 * 1024 * 1024
        ),
    )(
        panel_one,
        panel_two,
        inverse_one,
        inverse_two,
        targets.reshape(n_slots, size, size),
        column_blocks,
        row_map,
        rows_one.reshape(-1),
        cols_one.reshape(-1),
        rows_two.reshape(-1),
        cols_two.reshape(-1),
    )
    return lower_one, lower_two, trailing.reshape(targets.shape)


def solution(mesh):
    return jax.shard_map(
        per_device,
        mesh=mesh,
        in_specs=(
            P("col", "row"),
            P("col", "row"),
            P(),
            P(),
            P(),
            P("row"),
            P("row", "col", None, None, None),
            P("row", "col", None),
            P("row", "col", None),
            P("row", "col", None),
            P("row", "col", None),
        ),
        out_specs=(P("col", "row"), P("col", "row"), P("row", "col", None, None, None)),
        check_vma=False,
    )
```

```python
import functools
import heapq

import jax
import jax.numpy as jnp
from jax import lax
from jax.experimental import pallas as pl
from jax.experimental.pallas import tpu as pltpu
from jax.sharding import PartitionSpec as P

MESH = pl.DeviceIdType.MESH
NY, NZ, NX, NC = 4, 8, 4, 2

PART_A, HALF_A0, HALF_A1 = (0, 304), (0, 160), (160, 144)
PART_B, HALF_B0, HALF_B1 = (304, 208), (304, 112), (416, 96)
STEP = {"y+": (1, 0), "y-": (-1, 0), "z+": (0, 1), "z-": (0, -1)}
OWN_SENDS = (
    ("z+", PART_A),
    ("z-", PART_A),
    ("y+", PART_B),
    ("y-", PART_B),
    ("y+", PART_A),
    ("y-", PART_A),
    ("z+", PART_B),
    ("z-", PART_B),
)


def wrapped(value, size):
    value %= size
    return value - size if value > size // 2 else value


def next_source(source, way):
    dy, dz = STEP[way]
    return (wrapped(source[0] - dy, NY), wrapped(source[1] - dz, NZ))


def forwards(way, piece, source, seen):
    sy, sz = source
    if piece[0] < PART_A[1]:
        first, second = HALF_A0, HALF_A1
        if way[0] == "z":
            half = first if way == "z+" else second
            out = [(way, PART_A)] if abs(sz) < 3 else []
            if abs(sz) == 3:
                out.append((way, half))
            if abs(sz) < 4 or {first, second} <= seen:
                out += [("y+", PART_A), ("y-", PART_A)]
            return out
        return [(way, first if way == "y+" else second)] if abs(sy) == 1 else []
    first, second = HALF_B0, HALF_B1
    if way[0] == "y":
        out = []
        if abs(sy) == 1:
            out.append((way, first if way == "y+" else second))
        if abs(sy) == 1 or {first, second} <= seen:
            out += [("z+", PART_B), ("z-", PART_B)]
        return out
    if abs(sz) < 3:
        return [(way, PART_B)]
    return [(way, first if way == "z+" else second)] if abs(sz) == 3 else []


LINK_RATE, LATENCY, BACKLOG = 47.0, 2.0, 1.2


def hops_left(way, piece, source):
    sy, sz = next_source(source, way)
    if piece[0] < PART_A[1]:
        return 2 - abs(sy) if way[0] == "y" else 4 - abs(sz) + 2
    return 4 - abs(sz) if way[0] == "z" else 2 - abs(sy) + 4


def receives():
    found, heap = [], [(w, p, next_source((0, 0), w)) for w, p in OWN_SENDS]
    seen = {}
    while heap:
        way, piece, source = heap.pop(0)
        found.append((way, piece, source))
        seen.setdefault(source, set()).add(piece)
        for onward, part in forwards(way, piece, source, seen[source]):
            heap.append((onward, part, next_source(source, onward)))
    return found


EVENTS = receives()
EVENT = {event: i for i, event in enumerate(EVENTS)}
N_EVENTS = len(EVENTS)
VMEM_LIMIT = 26 * 1024 * 1024
FINISH_LIMIT = 6 * 1024 * 1024
CHAIN = (
    ("sum_y", None, 0.8, 0.15),
    ("sum_back", "sum_y", 5.3, 0.15),
    ("bridge_spread", "sum_back", 5.5, 0.05),
    ("one_1", None, 7.0, 0.02),
    ("one_3", None, 9.0, 0.02),
    ("one_2", None, 9.5, 0.02),
    ("one_side", "one_2", 2.2, 0.02),
    ("two_1", None, 12.0, 0.02),
    ("two_3", None, 13.0, 0.02),
    ("two_2", None, 15.5, 0.02),
    ("two_side", "two_2", 1.7, 0.02),
    ("bridge_1", "bridge_spread", 5.0, 0.02),
    ("bridge_3", "bridge_spread", 5.0, 0.02),
    ("bridge_2", "bridge_spread", 6.5, 0.02),
    ("bridge_side", "bridge_2", 1.7, 0.02),
)


def make_program():
    free = dict.fromkeys(STEP, 0.0)
    arriving, pending, seen, rows = [], {way: [] for way in STEP}, ({}, {}), ({}, {})
    ready = ([(0, 0)], [])
    program, ended, state = [], {}, {"now": 0.0, "count": 0, "products": [0, 0], "combined": 0}
    chain = list(CHAIN)

    def queue(p, way, piece, source):
        state["count"] += 1
        rank = (p, -hops_left(way, piece, source), state["count"])
        heapq.heappush(pending[way], (rank, p, piece, source))

    def ship(way):
        _, p, piece, source = heapq.heappop(pending[way])
        free[way] = max(free[way], state["now"]) + piece[1] * 256 / 1000 / LINK_RATE
        heapq.heappush(arriving, (free[way] + LATENCY, state["count"], p, way, piece, next_source(source, way)))
        state["count"] += 1
        program.append(("send", p, way, piece, source))
        state["now"] += 0.02

    def receive():
        _, _, p, way, piece, source = heapq.heappop(arriving)
        program.append(("wait", p, way, piece, source))
        state["now"] += 0.02
        seen[p].setdefault(source, set()).add(piece)
        rows[p][source] = rows[p].get(source, 0) + piece[1]
        for onward, part in forwards(way, piece, source, seen[p][source]):
            queue(p, onward, part, source)
        if rows[p][source] == 512:
            ready[p].append(source)

    steps = [("factor_one", i, 0.53, "one_side") for i in range(4)]
    steps += [("bridge_build", i, 0.5, "bridge_side") for i in range(4)]
    steps += [("factor_two", i, 0.86, "two_side") for i in range(4)]
    jobs = {name: [s for s in steps if s[0] == name] for name in ("factor_one", "bridge_build", "factor_two")}

    def job():
        for name, before in (("bridge_build", ()), ("factor_two", ("factor_one", "bridge_build")), ("factor_one", ())):
            if jobs[name] and not any(jobs[b] for b in before) and jobs[name][0][3] in ended:
                if ended[jobs[name][0][3]] <= state["now"] and (name != "factor_two" or "two_side" in ended):
                    _, i, cost, _ = jobs[name].pop(0)
                    return (name, i), cost
        if not jobs["factor_one"] and len(ready[0]) >= 2:
            return ("products", 0, ready[0].pop(0), ready[0].pop(0)), 0.65
        if state["products"][0] == 16 and state["combined"] < 8:
            state["combined"] += 1
            return ("combine", state["combined"] - 1), 0.32
        if state["combined"] == 8 and not jobs["factor_two"] and len(ready[1]) >= 2:
            return ("products", 1, ready[1].pop(0), ready[1].pop(0)), 0.65
        return None, 0.0

    def begin(p):
        for way, piece in OWN_SENDS:
            queue(p, way, piece, (0, 0))

    begin(0)
    while True:
        now = state["now"]
        if arriving and arriving[0][0] <= now:
            receive()
            continue
        ways = [w for w in STEP if pending[w] and free[w] - now < BACKLOG]
        if ways:
            ship(min(ways, key=lambda w: free[w]))
            continue
        due = [c for c in chain if (c[1] is None or c[1] in ended) and (ended.get(c[1], 0.0) + c[2] <= now)]
        if due:
            chain.remove(due[0])
            program.append(("chain", due[0][0]))
            state["now"] += due[0][3]
            ended[due[0][0]] = state["now"]
            continue
        work, cost = job()
        if work:
            program.append(("job",) + work)
            state["now"] += cost
            if work[0] == "products":
                state["products"][work[1]] += 1
            if work == ("factor_two", 0):
                ready[1].append((0, 0))
                begin(1)
            continue
        later = [arriving[0][0]] if arriving else []
        later += [free[w] - BACKLOG for w in STEP if pending[w]]
        later += [ended.get(c[1], 0.0) + c[2] for c in chain if c[1] is None or c[1] in ended]
        if not later:
            break
        state["now"] = max(now + 0.01, min(later))
    return program, state["now"]


PROGRAM, PLANNED = make_program()


def kernel(
    panel_one,
    panel_two,
    inverse_one,
    inverse_two,
    targets,
    column_blocks,
    row_map,
    rows_one,
    cols_one,
    lower_one,
    lower_two,
    upper,
    lower,
    partial,
    slab_one,
    slab_two,
    full_one,
    full_two,
    inv_one,
    inv_two,
    own_raw,
    pick,
    ring_z,
    mid,
    ring_y,
    raw_bridge,
    bridge_t,
    blocks_one,
    blocks_two,
    left_one,
    left_two,
    tiles,
    staged,
    bridge_from,
    map_from,
    pick_rows,
    pick_cols,
    local_sem,
    index_sem,
    x_send,
    x_recv,
    side_recv,
    swap_send,
    swap_recv,
    sum_send,
    sum_recv,
    tile_send,
    tile_recv,
):
    f32, bf16 = jnp.float32, jnp.bfloat16
    row, col = lax.axis_index("row"), lax.axis_index("col")
    y, z = row // NZ, row % NZ
    x, core = col // NC, col % NC
    slab = slab_one.shape[1]
    base = pl.multiple_of(col * slab, slab)

    def row_at(dy, dz):
        return ((y + dy + NY) % NY) * NZ + (z + dz + NZ) % NZ

    def col_at(dx):
        return ((x + dx) % NX) * NC + core

    partner = x * NC + (1 - core)

    def remote(src, dst, send, recv, device):
        return pltpu.make_async_remote_copy(
            src_ref=src, dst_ref=dst, send_sem=send, recv_sem=recv, device_id=device, device_id_type=MESH
        )

    def await_recv(ref, sem):
        remote(ref, ref, tile_send.at[0], sem, (row, partner)).wait_recv()

    def await_send(ref, sem):
        remote(ref, ref, sem, tile_recv.at[0, 0], (row, partner)).wait_send()

    loads = []
    n_blocks = slab_one.shape[0]
    for which, (panel, mine) in enumerate(((panel_one, slab_one), (panel_two, slab_two))):
        for j in range(n_blocks):
            loads.append(pltpu.make_async_copy(panel.at[:, pl.ds(j * 128, 128)], mine.at[j], local_sem.at[which]))
    for copy in loads:
        copy.start()
    load_inv_one = pltpu.make_async_copy(inverse_one, inv_one, local_sem.at[2])
    load_inv_two = pltpu.make_async_copy(inverse_two, inv_two, local_sem.at[3])
    load_targets = pltpu.make_async_copy(targets, staged, local_sem.at[4])
    small = [(column_blocks, bridge_from), (row_map, map_from), (rows_one, pick_rows), (cols_one, pick_cols)]
    small = [pltpu.make_async_copy(src, dst, index_sem.at[i]) for i, (src, dst) in enumerate(small)]
    for copy in small:
        copy.start()
    load_inv_one.start()
    load_inv_two.start()
    load_targets.start()

    barrier = pltpu.get_barrier_semaphore()
    in_row = [(row, (col + d) % (NX * NC)) for d in range(1, NX * NC)]
    along_z = [(row_at(0, d), col) for d in range(1, NZ)]
    along_y = [(row_at(d, 0), col) for d in range(1, NY)]
    for device in in_row + along_z + along_y:
        pl.semaphore_signal(barrier, inc=1, device_id=device, device_id_type=MESH)
    for copy in small:
        copy.wait()
    pltpu.make_async_copy(slab_one, slab_one, local_sem.at[0]).wait()
    pltpu.make_async_copy(slab_two, slab_two, local_sem.at[1]).wait()
    keep_one = pltpu.make_async_copy(slab_one, full_one.at[:, pl.ds(base, slab), :], local_sem.at[5])
    keep_two = pltpu.make_async_copy(slab_two, full_two.at[:, pl.ds(base, slab), :], local_sem.at[6])
    keep_raw = pltpu.make_async_copy(slab_one.at[col], own_raw.at[pl.ds(base, slab), :], local_sem.at[7])
    keep_one.start()
    keep_two.start()
    keep_raw.start()
    pl.semaphore_wait(barrier, len(in_row) + len(along_z) + len(along_y))

    for _, peer in in_row:
        remote(
            slab_one.at[peer], own_raw.at[pl.ds(base, slab), :], swap_send, swap_recv, (row, peer)
        ).start()

    for k in range(4):
        chosen = bridge_from[k]
        block = slab_one[chosen % n_blocks]
        block = jnp.where(chosen // n_blocks == row, block.astype(f32), 0.0).astype(bf16)
        pick[2 * k] = block[:32]
        pick[2 * k + 1] = block[32:]

    def spread(mine, full, which):
        for dx in range(1, NX):
            remote(
                mine, full.at[:, pl.ds(base, slab), :], x_send.at[which], x_recv.at[which, dx - 1], (row, col_at(dx))
            ).start()
        remote(
            mine, full.at[:, pl.ds(base, slab), :], x_send.at[which], side_recv.at[which], (row, partner)
        ).start()

    def pass_on(full, which, dx):
        ref = full.at[:, pl.ds(pl.multiple_of(col_at(NX - dx) * slab, slab), slab), :]
        await_recv(ref, x_recv.at[which, dx - 1])
        remote(ref, ref, x_send.at[which], side_recv.at[which], (row, partner)).start()

    def side_wait(full, which):
        await_recv(full.at[:, pl.ds(0, NX * slab), :], side_recv.at[which])

    def sum_z_send():
        for d in range(1, NZ):
            remote(
                pick.at[(z + d) % NZ], ring_z.at[d - 1], sum_send.at[0], sum_recv.at[0], (row_at(0, d), col)
            ).start()

    piece_k = z // 2
    piece_rows = pl.ds(pl.multiple_of(base + 32 * (z % 2), 32), 32)

    def sum_y_send():
        await_recv(ring_z, sum_recv.at[0])
        total = pick[z].astype(f32)
        for d in range(NZ - 1):
            total += ring_z[d].astype(f32)
        mid[...] = total.astype(bf16)
        for d in range(1, NY):
            remote(mid, ring_y.at[d - 1], sum_send.at[1], sum_recv.at[1], (row_at(d, 0), col)).start()

    def sum_z_return():
        await_recv(ring_y, sum_recv.at[1])
        total = mid[...].astype(f32)
        for d in range(NY - 1):
            total += ring_y[d].astype(f32)
        raw_bridge[piece_k, piece_rows, :] = total.astype(bf16)
        ref = raw_bridge.at[piece_k, piece_rows, :]
        for d in range(1, NZ):
            remote(ref, ref, sum_send.at[2], sum_recv.at[2], (row_at(0, d), col)).start()

    def bridge_spread():
        await_recv(ring_z, sum_recv.at[2])
        spread(raw_bridge.at[:, pl.ds(base, slab), :], raw_bridge, 2)

    def tile_copy(p, way, piece, source):
        ref = tiles.at[p, row_at(*source), pl.ds(*piece), :]
        event = EVENT[(way, piece, next_source(source, way))]
        remote(ref, ref, tile_send.at[p], tile_recv.at[p, event], (row_at(*STEP[way]), col)).start()

    def tile_wait(p, way, piece, source):
        ref = tiles.at[p, row_at(*source), pl.ds(*piece), :]
        await_recv(ref, tile_recv.at[p, EVENT[(way, piece, source)]])

    def dot(a, b):
        return jnp.dot(a, b, preferred_element_type=f32)

    def first_block():
        await_recv(own_raw.at[pl.ds(0, (NX * NC - 1) * slab), :], swap_recv)
        tiles[0, row] = dot(inv_one[...], own_raw[...]).astype(bf16)

    def store_pair(blocks, left, i, value):
        for h in range(2):
            part = value[:, h * 128 : (h + 1) * 128]
            blocks[2 * i + h] = part.astype(bf16)
            left[pl.ds(pl.multiple_of((2 * i + h) * 128, 128), 128), :] = part.T.astype(bf16)

    def factor_one(i):
        pair = jnp.concatenate([full_one[2 * i], full_one[2 * i + 1]], axis=1)
        store_pair(blocks_one, left_one, i, dot(inv_one[...], pair))
        if i == n_blocks // 2 - 1:
            write_lower(blocks_one, lower_one)

    def bridge_build(k):
        value = dot(inv_one[...], raw_bridge[k])
        bridge_t[k * 128 : (k + 1) * 128, :] = value.T.astype(bf16)

    def pair_two(i):
        mapped = jnp.concatenate(
            [blocks_one[map_from[2 * i] % n_blocks], blocks_one[map_from[2 * i + 1] % n_blocks]], axis=1
        )
        pair = jnp.concatenate([full_two[2 * i], full_two[2 * i + 1]], axis=1)
        updated = (pair.astype(f32) - dot(bridge_t[...], mapped)).astype(bf16)
        store_pair(blocks_two, left_two, i, dot(inv_two[...], updated))

    def factor_two(i):
        pair_two((col // 2 + i) % (n_blocks // 2))
        if i == 0:
            tiles[1, row] = blocks_two[col]
        if i == n_blocks // 2 - 1:
            write_lower(blocks_two, lower_two)

    def products_of(p, first, second):
        left = (left_one, left_two)[p]
        t0, t1 = row_at(*first), row_at(*second)

        @pl.loop(0, 2)
        def _(m):
            pair = jnp.concatenate([tiles[p, t0], tiles[p, t1]], axis=1)
            value = dot(left[pl.ds(pl.multiple_of(m * 512, 512), 512), :], pair)
            for h, t in enumerate((t0, t1)):
                part = value[:, h * 128 : (h + 1) * 128].reshape(4, 128, 128)
                upper[pl.ds(t * n_blocks + 4 * m, 4)] = part[:, :64]
                lower[pl.ds(t * n_blocks + 4 * m, 4)] = part[:, 64:]

    n_slots = staged.shape[0]

    def combine(g):
        if g == 0:
            load_targets.wait()

        @pl.loop(g * n_slots // 8, (g + 1) * n_slots // 8, unroll=4)
        def _(s):
            index = (pick_cols[s] // n_blocks) * n_blocks + pick_rows[s] % n_blocks
            partial[s, :64] = staged[s, :64].astype(f32) - upper[index]
            partial[s, 64:] = staged[s, 64:].astype(f32) - lower[index]

    def write_lower(blocks, out):
        for j in range(n_blocks):
            out[:, j * 128 : (j + 1) * 128] = blocks[j, pl.ds(base, slab), :]

    chain = {
        "sum_y": sum_y_send,
        "sum_back": sum_z_return,
        "bridge_spread": bridge_spread,
        "one_side": lambda: side_wait(full_one, 0),
        "two_side": lambda: side_wait(full_two, 1),
        "bridge_side": lambda: side_wait(raw_bridge, 2),
    }
    for which, (name, full) in enumerate((("one", full_one), ("two", full_two), ("bridge", raw_bridge))):
        for dx in range(1, NX):
            chain[f"{name}_{dx}"] = functools.partial(pass_on, full, which, dx)
    jobs = {
        "factor_one": factor_one,
        "bridge_build": bridge_build,
        "factor_two": factor_two,
        "products": products_of,
        "combine": combine,
    }

    sum_z_send()
    load_inv_one.wait()
    load_inv_two.wait()
    keep_raw.wait()
    keep_one.wait()
    keep_two.wait()
    first_block()
    started = False
    for kind, *what in PROGRAM:
        if kind == "send":
            tile_copy(*what)
        elif kind == "wait":
            if not started:
                spread(slab_one, full_one, 0)
                spread(slab_two, full_two, 1)
                started = True
            tile_wait(*what)
        elif kind == "chain":
            chain[what[0]]()
        else:
            jobs[what[0]](*what[1:])

    await_send(own_raw.at[pl.ds(0, (NX * NC - 1) * slab), :], swap_send)
    await_send(ring_z, sum_send.at[0])
    await_send(ring_y, sum_send.at[1])
    await_send(ring_z, sum_send.at[2])
    await_send(full_one.at[pl.ds(0, n_blocks - 1)], x_send.at[0])
    await_send(full_two.at[pl.ds(0, n_blocks - 1)], x_send.at[1])
    await_send(full_two.at[pl.ds(0, n_blocks - 1), pl.ds(0, 256), :], x_send.at[2])
    await_send(tiles.at[0, pl.ds(0, NY * NZ - 1)], tile_send.at[0])
    await_send(tiles.at[1, pl.ds(0, NY * NZ - 1)], tile_send.at[1])


GROUP = 16


def finish_kernel(
    rows_in, cols_in, lower_one, lower_two, upper, lower, partial, out_one, out_two, trailing, staged, rows, cols, sem
):
    index = [pltpu.make_async_copy(rows_in, rows, sem.at[2]), pltpu.make_async_copy(cols_in, cols, sem.at[3])]
    for copy in index:
        copy.start()
    n_slots = partial.shape[0]
    n_blocks = lower_one.shape[1] // partial.shape[-1]
    copies = [
        pltpu.make_async_copy(lower_one, out_one, sem.at[0]),
        pltpu.make_async_copy(lower_two, out_two, sem.at[1]),
    ]
    for copy in copies:
        copy.start()
    for copy in index:
        copy.wait()
    for g in range(n_slots // GROUP):

        @pl.loop(g * GROUP, (g + 1) * GROUP, unroll=4)
        def _(s):
            index = (cols[s] // n_blocks) * n_blocks + rows[s] % n_blocks
            staged[s, :64] = (partial[s, :64] - upper[index]).astype(staged.dtype)
            staged[s, 64:] = (partial[s, 64:] - lower[index]).astype(staged.dtype)

        part = pl.ds(g * GROUP, GROUP)
        copies.append(pltpu.make_async_copy(staged.at[part], trailing.at[part], sem.at[4 + g]))
        copies[-1].start()
    for copy in copies:
        copy.wait()


def per_device(
    panel_one,
    panel_two,
    inverse_one,
    inverse_two,
    column_blocks,
    row_map,
    targets,
    rows_one,
    cols_one,
    rows_two,
    cols_two,
):
    slab, row_count = panel_one.shape
    width = inverse_one.shape[0]
    size = targets.shape[-1]
    n_slots = targets.shape[2]
    n_blocks = row_count // size
    n_rows = NY * NZ
    bf16, f32 = jnp.bfloat16, jnp.float32
    vmem = pltpu.VMEM
    dma = pltpu.SemaphoreType.DMA
    in_hbm = pl.BlockSpec(memory_space=pltpu.HBM)
    smem = pltpu.SMEM
    in_vmem = pl.BlockSpec(memory_space=vmem)

    def stay(*arrays):
        return [pltpu.with_memory_space_constraint(array, pltpu.HBM) for array in arrays]

    held = pl.pallas_call(
        kernel,
        out_shape=(
            vmem(panel_one.shape, bf16),
            vmem(panel_two.shape, bf16),
            vmem((n_rows * n_blocks, size // 2, size), f32),
            vmem((n_rows * n_blocks, size // 2, size), f32),
            vmem((n_slots, size, size), f32),
        ),
        in_specs=[in_hbm] * 9,
        out_specs=(in_vmem,) * 5,
        scratch_shapes=[
            vmem((n_blocks, slab, size), bf16),
            vmem((n_blocks, slab, size), bf16),
            vmem((n_blocks, width, size), bf16),
            vmem((n_blocks, width, size), bf16),
            vmem((width, width), bf16),
            vmem((width, width), bf16),
            vmem((width, size), bf16),
            vmem((8, 32, size), bf16),
            vmem((NZ - 1, 32, size), bf16),
            vmem((32, size), bf16),
            vmem((NY - 1, 32, size), bf16),
            vmem((4, width, size), bf16),
            vmem((width, width), bf16),
            vmem((n_blocks, width, size), bf16),
            vmem((n_blocks, width, size), bf16),
            vmem((row_count, width), bf16),
            vmem((row_count, width), bf16),
            vmem((2, n_rows, width, size), bf16),
            vmem((n_slots, size, size), bf16),
            smem((4,), jnp.int32),
            smem((n_blocks,), jnp.int32),
            smem((n_slots,), jnp.int32),
            smem((n_slots,), jnp.int32),
            dma((8,)),
            dma((4,)),
            dma((3,)),
            dma((3, NX - 1)),
            dma((3,)),
            dma,
            dma,
            dma((3,)),
            dma((3,)),
            dma((2,)),
            dma((2, N_EVENTS)),
        ],
        compiler_params=pltpu.CompilerParams(
            collective_id=0, has_side_effects=True, vmem_limit_bytes=VMEM_LIMIT
        ),
    )(
        *stay(
            panel_one,
            panel_two,
            inverse_one,
            inverse_two,
            targets.reshape(n_slots, size, size),
            column_blocks,
            row_map,
            rows_one.reshape(-1),
            cols_one.reshape(-1),
        )
    )
    lower_one, lower_two, trailing = pl.pallas_call(
        finish_kernel,
        out_shape=(
            jax.ShapeDtypeStruct(panel_one.shape, bf16),
            jax.ShapeDtypeStruct(panel_two.shape, bf16),
            jax.ShapeDtypeStruct((n_slots, size, size), bf16),
        ),
        in_specs=[in_hbm] * 2 + [in_vmem] * 5,
        out_specs=(in_hbm,) * 3,
        scratch_shapes=[
            vmem((n_slots, size, size), bf16),
            smem((n_slots,), jnp.int32),
            smem((n_slots,), jnp.int32),
            dma((4 + n_slots // GROUP,)),
        ],
        compiler_params=pltpu.CompilerParams(vmem_limit_bytes=FINISH_LIMIT),
    )(*stay(rows_two.reshape(-1), cols_two.reshape(-1)), *held)
    return lower_one, lower_two, trailing.reshape(targets.shape)


def solution(mesh):
    return jax.shard_map(
        per_device,
        mesh=mesh,
        in_specs=(
            P("col", "row"),
            P("col", "row"),
            P(),
            P(),
            P(),
            P("row"),
            P("row", "col", None, None, None),
            P("row", "col", None),
            P("row", "col", None),
            P("row", "col", None),
            P("row", "col", None),
        ),
        out_specs=(P("col", "row"), P("col", "row"), P("row", "col", None, None, None)),
        check_vma=False,
    )
```

```python
import functools
import heapq

import jax
import jax.numpy as jnp
from jax import lax
from jax.experimental import pallas as pl
from jax.experimental.pallas import tpu as pltpu
from jax.sharding import PartitionSpec as P

MESH = pl.DeviceIdType.MESH
NY, NZ, NX, NC = 4, 8, 4, 2

PART_A, HALF_A0, HALF_A1 = (0, 304), (0, 160), (160, 144)
PART_B, HALF_B0, HALF_B1 = (304, 208), (304, 112), (416, 96)
STEP = {"y+": (1, 0), "y-": (-1, 0), "z+": (0, 1), "z-": (0, -1)}
OWN_SENDS = (
    ("z+", PART_A),
    ("z-", PART_A),
    ("y+", PART_B),
    ("y-", PART_B),
    ("y+", PART_A),
    ("y-", PART_A),
    ("z+", PART_B),
    ("z-", PART_B),
)


def wrapped(value, size):
    value %= size
    return value - size if value > size // 2 else value


def next_source(source, way):
    dy, dz = STEP[way]
    return (wrapped(source[0] - dy, NY), wrapped(source[1] - dz, NZ))


def forwards(way, piece, source, seen):
    sy, sz = source
    if piece[0] < PART_A[1]:
        first, second = HALF_A0, HALF_A1
        if way[0] == "z":
            half = first if way == "z+" else second
            out = [(way, PART_A)] if abs(sz) < 3 else []
            if abs(sz) == 3:
                out.append((way, half))
            if abs(sz) < 4 or {first, second} <= seen:
                out += [("y+", PART_A), ("y-", PART_A)]
            return out
        return [(way, first if way == "y+" else second)] if abs(sy) == 1 else []
    first, second = HALF_B0, HALF_B1
    if way[0] == "y":
        out = []
        if abs(sy) == 1:
            out.append((way, first if way == "y+" else second))
        if abs(sy) == 1 or {first, second} <= seen:
            out += [("z+", PART_B), ("z-", PART_B)]
        return out
    if abs(sz) < 3:
        return [(way, PART_B)]
    return [(way, first if way == "z+" else second)] if abs(sz) == 3 else []


LINK_RATE, LATENCY, BACKLOG, PANEL_WEIGHT = 47.0, 2.6, 0.6, 100.0


def hops_left(way, piece, source):
    sy, sz = next_source(source, way)
    if piece[0] < PART_A[1]:
        return 2 - abs(sy) if way[0] == "y" else 4 - abs(sz) + 2
    return 4 - abs(sz) if way[0] == "z" else 2 - abs(sy) + 4


def receives():
    found, heap = [], [(w, p, next_source((0, 0), w)) for w, p in OWN_SENDS]
    seen = {}
    while heap:
        way, piece, source = heap.pop(0)
        found.append((way, piece, source))
        seen.setdefault(source, set()).add(piece)
        for onward, part in forwards(way, piece, source, seen[source]):
            heap.append((onward, part, next_source(source, onward)))
    return found


EVENTS = receives()
EVENT = {event: i for i, event in enumerate(EVENTS)}
N_EVENTS = len(EVENTS)
VMEM_LIMIT = 34 * 1024 * 1024
FINISH_LIMIT = 6 * 1024 * 1024
CHAIN = (
    ("sum_back", None, 3.9, 0.15),
    ("bridge_spread", "sum_back", 5.8, 0.05),
    ("one_1", None, 6.0, 0.02),
    ("one_3", None, 6.0, 0.02),
    ("one_2", None, 10.2, 0.02),
    ("one_side", "one_2", 2.8, 0.02),
    ("two_1", None, 9.0, 0.02),
    ("two_3", None, 9.0, 0.02),
    ("two_2", None, 12.5, 0.02),
    ("two_side", "two_2", 2.8, 0.02),
    ("bridge_1", "bridge_spread", 4.3, 0.02),
    ("bridge_3", "bridge_spread", 4.3, 0.02),
    ("bridge_2", "bridge_3", 3.3, 0.02),
    ("bridge_side", "bridge_2", 2.0, 0.02),
)


def make_program():
    free = dict.fromkeys(STEP, 0.0)
    arriving, pending, seen, rows = [], {way: [] for way in STEP}, ({}, {}), ({}, {})
    ready = ([(0, 0)], [])
    program, ended, state = [], {}, {"now": 0.0, "count": 0, "products": [0, 0], "combined": 0}
    chain = list(CHAIN)

    def queue(p, way, piece, source):
        state["count"] += 1
        rank = (PANEL_WEIGHT * p - hops_left(way, piece, source), state["count"])
        heapq.heappush(pending[way], (rank, p, piece, source))

    def ship(way):
        _, p, piece, source = heapq.heappop(pending[way])
        free[way] = max(free[way], state["now"]) + piece[1] * 256 / 1000 / LINK_RATE
        heapq.heappush(arriving, (free[way] + LATENCY, state["count"], p, way, piece, next_source(source, way)))
        state["count"] += 1
        program.append(("send", p, way, piece, source))
        state["now"] += 0.02

    def receive():
        _, _, p, way, piece, source = heapq.heappop(arriving)
        program.append(("wait", p, way, piece, source))
        state["now"] += 0.02
        seen[p].setdefault(source, set()).add(piece)
        rows[p][source] = rows[p].get(source, 0) + piece[1]
        for onward, part in forwards(way, piece, source, seen[p][source]):
            queue(p, onward, part, source)
        if rows[p][source] == 512:
            ready[p].append(source)

    steps = [("factor_one", i, 0.53, "one_side") for i in range(4)]
    steps += [("bridge_build", i, 0.55, "bridge_side") for i in range(2)]
    steps += [("factor_two", i, 0.86, "two_side") for i in range(4)]
    jobs = {name: [s for s in steps if s[0] == name] for name in ("factor_one", "bridge_build", "factor_two")}

    def job():
        for name, before in (("bridge_build", ()), ("factor_two", ("factor_one", "bridge_build")), ("factor_one", ())):
            if jobs[name] and not any(jobs[b] for b in before) and jobs[name][0][3] in ended:
                if ended[jobs[name][0][3]] <= state["now"] and (name != "factor_two" or "two_side" in ended):
                    _, i, cost, _ = jobs[name].pop(0)
                    return (name, i), cost
        free_to_run = (not jobs["factor_one"], state["combined"] == 8 and not jobs["factor_two"])
        for p in range(2):
            if free_to_run[p] and len(ready[p]) >= 2:
                return ("products", p) + (ready[p].pop(0), ready[p].pop(0)), 0.52
            if p == 0 and state["products"][0] == 32 and state["combined"] < 8:
                state["combined"] += 1
                return ("combine", state["combined"] - 1), 0.2
        return None, 0.0

    def begin(p):
        for way, piece in OWN_SENDS:
            queue(p, way, piece, (0, 0))

    begin(0)
    while True:
        now = state["now"]
        if arriving and arriving[0][0] <= now:
            receive()
            continue
        ways = [w for w in STEP if pending[w] and free[w] - now < BACKLOG]
        if ways:
            ship(min(ways, key=lambda w: free[w]))
            continue
        due = [c for c in chain if (c[1] is None or c[1] in ended) and (ended.get(c[1], 0.0) + c[2] <= now)]
        if due:
            chain.remove(due[0])
            program.append(("chain", due[0][0]))
            state["now"] += due[0][3]
            ended[due[0][0]] = state["now"]
            continue
        work, cost = job()
        if work:
            program.append(("job",) + work)
            state["now"] += cost
            if work[0] == "products":
                state["products"][work[1]] += len(work) - 2
            if work == ("factor_two", 0):
                ready[1].append((0, 0))
                begin(1)
            continue
        later = [arriving[0][0]] if arriving else []
        later += [free[w] - BACKLOG for w in STEP if pending[w]]
        later += [ended.get(c[1], 0.0) + c[2] for c in chain if c[1] is None or c[1] in ended]
        if not later:
            break
        state["now"] = max(now + 0.01, min(later))
    return program, state["now"]


PROGRAM, PLANNED = make_program()


def kernel(
    panel_one,
    panel_two,
    inverse_one,
    inverse_two,
    targets,
    column_blocks,
    row_map,
    rows_one,
    cols_one,
    lower_one,
    lower_two,
    upper,
    lower,
    partial,
    slab_one,
    slab_two,
    full_one,
    full_two,
    inv_one,
    inv_two,
    own_raw,
    pick,
    ring_z,
    mid,
    ring_y,
    raw_bridge,
    bridge_t,
    blocks_one,
    blocks_two,
    left,
    tiles,
    staged,
    bridge_from,
    map_from,
    pick_rows,
    pick_cols,
    local_sem,
    index_sem,
    x_send,
    x_recv,
    side_recv,
    swap_send,
    swap_recv,
    sum_send,
    sum_recv,
    tile_send,
    tile_recv,
):
    f32, bf16 = jnp.float32, jnp.bfloat16
    row, col = lax.axis_index("row"), lax.axis_index("col")
    y, z = row // NZ, row % NZ
    x, core = col // NC, col % NC
    slab = slab_one.shape[1]
    base = pl.multiple_of(col * slab, slab)

    def row_at(dy, dz):
        return ((y + dy + NY) % NY) * NZ + (z + dz + NZ) % NZ

    def col_at(dx):
        return ((x + dx) % NX) * NC + core

    partner = x * NC + (1 - core)

    def remote(src, dst, send, recv, device):
        return pltpu.make_async_remote_copy(
            src_ref=src, dst_ref=dst, send_sem=send, recv_sem=recv, device_id=device, device_id_type=MESH
        )

    def await_recv(ref, sem):
        remote(ref, ref, tile_send.at[0], sem, (row, partner)).wait_recv()

    def await_send(ref, sem):
        remote(ref, ref, sem, tile_recv.at[0, 0], (row, partner)).wait_send()

    loads = []
    n_blocks = slab_one.shape[0]
    for which, (panel, mine) in enumerate(((panel_one, slab_one), (panel_two, slab_two))):
        for j in range(n_blocks):
            loads.append(pltpu.make_async_copy(panel.at[:, pl.ds(j * 128, 128)], mine.at[j], local_sem.at[which]))
    for copy in loads:
        copy.start()
    load_inv_one = pltpu.make_async_copy(inverse_one, inv_one, local_sem.at[2])
    load_inv_two = pltpu.make_async_copy(inverse_two, inv_two, local_sem.at[3])
    load_targets = pltpu.make_async_copy(targets, staged, local_sem.at[4])
    small = [(column_blocks, bridge_from), (row_map, map_from), (rows_one, pick_rows), (cols_one, pick_cols)]
    small = [pltpu.make_async_copy(src, dst, index_sem.at[i]) for i, (src, dst) in enumerate(small)]
    for copy in small:
        copy.start()
    load_inv_one.start()
    load_inv_two.start()
    load_targets.start()

    barrier = pltpu.get_barrier_semaphore()
    in_row = [(row, (col + d) % (NX * NC)) for d in range(1, NX * NC)]
    along_z = [(row_at(0, d), col) for d in range(1, NZ)]
    along_y = [(row_at(d, 0), col) for d in range(1, NY)]
    for device in in_row + along_z + along_y:
        pl.semaphore_signal(barrier, inc=1, device_id=device, device_id_type=MESH)
    for copy in small:
        copy.wait()
    pltpu.make_async_copy(slab_one, slab_one, local_sem.at[0]).wait()
    pltpu.make_async_copy(slab_two, slab_two, local_sem.at[1]).wait()
    keep_one = pltpu.make_async_copy(slab_one, full_one.at[:, pl.ds(base, slab), :], local_sem.at[5])
    keep_two = pltpu.make_async_copy(slab_two, full_two.at[:, pl.ds(base, slab), :], local_sem.at[6])
    keep_raw = pltpu.make_async_copy(slab_one.at[col], own_raw.at[pl.ds(base, slab), :], local_sem.at[7])
    keep_one.start()
    keep_two.start()
    keep_raw.start()
    pl.semaphore_wait(barrier, len(in_row) + len(along_z) + len(along_y))

    for _, peer in in_row:
        remote(
            slab_one.at[peer], own_raw.at[pl.ds(base, slab), :], swap_send, swap_recv, (row, peer)
        ).start()

    for k in range(4):
        chosen = bridge_from[k]
        block = slab_one[chosen % n_blocks]
        block = jnp.where(chosen // n_blocks == row, block.astype(f32), 0.0).astype(bf16)
        pick[2 * k] = block[:32]
        pick[2 * k + 1] = block[32:]

    def slab_of(full, dx):
        return full.at[:, pl.ds(pl.multiple_of(col_at(NX - dx) * slab, slab), slab), :]

    def spread(mine, full, which):
        place = full.at[:, pl.ds(base, slab), :]
        for dx in (1, 3):
            remote(mine, place, x_send.at[which], x_recv.at[which, dx - 1], (row, col_at(dx))).start()
        remote(mine, place, x_send.at[which], side_recv.at[which], (row, partner)).start()

    def pass_on(full, which, dx):
        ref = slab_of(full, dx)
        half = full.shape[0] // 2
        if dx == 2:
            await_recv(ref.at[pl.ds(0, half)], x_recv.at[which, 1])
            await_recv(ref.at[pl.ds(half, half)], x_recv.at[which, 3])
        else:
            await_recv(ref, x_recv.at[which, dx - 1])
            part = ref.at[pl.ds(0 if dx == 1 else half, half)]
            remote(
                part, part, x_send.at[which], x_recv.at[which, 1 if dx == 1 else 3], (row, col_at(dx))
            ).start()
        remote(ref, ref, x_send.at[which], side_recv.at[which], (row, partner)).start()

    def side_wait(full, which):
        await_recv(full.at[:, pl.ds(0, NX * slab), :], side_recv.at[which])

    def sum_z_send():
        for d in range(1, NZ):
            remote(
                pick.at[(z + d) % NZ], ring_z.at[d - 1], sum_send.at[0], sum_recv.at[0], (row_at(0, d), col)
            ).start()

    piece_k = z // 2
    piece_rows = pl.ds(pl.multiple_of(base + 32 * (z % 2), 32), 32)

    def sum_y_send():
        await_recv(ring_z, sum_recv.at[0])
        total = pick[z].astype(f32)
        for d in range(NZ - 1):
            total += ring_z[d].astype(f32)
        mid[...] = total.astype(bf16)
        for d in range(1, NY):
            remote(mid, ring_y.at[d - 1], sum_send.at[1], sum_recv.at[1], (row_at(d, 0), col)).start()

    def sum_z_return():
        await_recv(ring_y, sum_recv.at[1])
        total = mid[...].astype(f32)
        for d in range(NY - 1):
            total += ring_y[d].astype(f32)
        raw_bridge[piece_k, piece_rows, :] = total.astype(bf16)
        ref = raw_bridge.at[piece_k, piece_rows, :]
        for d in range(1, NZ):
            remote(ref, ref, sum_send.at[2], sum_recv.at[2], (row_at(0, d), col)).start()

    def bridge_spread():
        await_recv(ring_z, sum_recv.at[2])
        spread(raw_bridge.at[:, pl.ds(base, slab), :], raw_bridge, 2)

    def tile_copy(p, way, piece, source):
        ref = tiles.at[p, row_at(*source), pl.ds(*piece), :]
        event = EVENT[(way, piece, next_source(source, way))]
        remote(ref, ref, tile_send.at[p], tile_recv.at[p, event], (row_at(*STEP[way]), col)).start()

    def tile_wait(p, way, piece, source):
        ref = tiles.at[p, row_at(*source), pl.ds(*piece), :]
        await_recv(ref, tile_recv.at[p, EVENT[(way, piece, source)]])

    def dot(a, b):
        return jnp.dot(a, b, preferred_element_type=f32)

    def first_block():
        await_recv(own_raw.at[pl.ds(0, (NX * NC - 1) * slab), :], swap_recv)
        tiles[0, row] = dot(inv_one[...], own_raw[...]).astype(bf16)

    def store_pair(blocks, p, i, value):
        for h in range(2):
            part = value[:, h * 128 : (h + 1) * 128]
            blocks[2 * i + h] = part.astype(bf16)
            left[p, pl.ds(pl.multiple_of((2 * i + h) * 128, 128), 128), :] = part.T.astype(bf16)

    def factor_one(i):
        pair = jnp.concatenate([full_one[2 * i], full_one[2 * i + 1]], axis=1)
        store_pair(blocks_one, 0, i, dot(inv_one[...], pair))
        if i == n_blocks // 2 - 1:
            write_lower(blocks_one, lower_one)

    def bridge_build(i):
        pair = jnp.concatenate([raw_bridge[2 * i], raw_bridge[2 * i + 1]], axis=1)
        bridge_t[i * 256 : (i + 1) * 256, :] = dot(inv_one[...], pair).T.astype(bf16)

    def pair_two(i):
        mapped = jnp.concatenate(
            [blocks_one[map_from[2 * i] % n_blocks], blocks_one[map_from[2 * i + 1] % n_blocks]], axis=1
        )
        pair = jnp.concatenate([full_two[2 * i], full_two[2 * i + 1]], axis=1)
        updated = (pair.astype(f32) - dot(bridge_t[...], mapped)).astype(bf16)
        store_pair(blocks_two, 1, i, dot(inv_two[...], updated))

    def factor_two(i):
        pair_two((col // 2 + i) % (n_blocks // 2))
        if i == 0:
            tiles[1, row] = blocks_two[col]
        if i == n_blocks // 2 - 1:
            write_lower(blocks_two, lower_two)

    def products_of(p, rows):
        value = dot(left[p], jnp.concatenate([tiles[p, t] for t in rows], axis=1))
        for h, t in enumerate(rows):
            part = value[:, h * 128 : (h + 1) * 128].reshape(n_blocks, 128, 128)
            upper[pl.ds(t * n_blocks, n_blocks)] = part[:, :64]
            lower[pl.ds(t * n_blocks, n_blocks)] = part[:, 64:]

    n_slots = staged.shape[0]

    def combine(g):
        if g == 0:
            load_targets.wait()

        @pl.loop(g * n_slots // 8, (g + 1) * n_slots // 8, unroll=4)
        def _(s):
            index = (pick_cols[s] // n_blocks) * n_blocks + pick_rows[s] % n_blocks
            partial[s, :64] = staged[s, :64].astype(f32) - upper[index]
            partial[s, 64:] = staged[s, 64:].astype(f32) - lower[index]

    def write_lower(blocks, out):
        for j in range(n_blocks):
            out[:, j * 128 : (j + 1) * 128] = blocks[j, pl.ds(base, slab), :]

    chain = {
        "sum_back": sum_z_return,
        "bridge_spread": bridge_spread,
        "one_side": lambda: side_wait(full_one, 0),
        "two_side": lambda: side_wait(full_two, 1),
        "bridge_side": lambda: side_wait(raw_bridge, 2),
    }
    for which, (name, full) in enumerate((("one", full_one), ("two", full_two), ("bridge", raw_bridge))):
        for dx in range(1, NX):
            chain[f"{name}_{dx}"] = functools.partial(pass_on, full, which, dx)
    jobs = {
        "factor_one": factor_one,
        "bridge_build": bridge_build,
        "factor_two": factor_two,
        "combine": combine,
    }

    sum_z_send()
    load_inv_one.wait()
    load_inv_two.wait()
    keep_raw.wait()
    keep_one.wait()
    keep_two.wait()
    first_block()
    sum_y_send()
    cuts, chosen = [[]], []
    for op in PROGRAM:
        if op[:2] == ("job", "products"):
            chosen.append(op[3:])
            cuts.append([])
        else:
            cuts[-1].append(op)
    cuts.pop()

    def run(ops):
        for kind, *what in ops:
            if kind == "send":
                tile_copy(*what)
            elif kind == "wait":
                tile_wait(*what)
            elif kind == "chain":
                chain[what[0]]()
            else:
                jobs[what[0]](*what[1:])

    def run_cut(i, first, last):
        if last - first == 1:
            run(cuts[first])
            return tuple(row_at(*source) for source in chosen[first])
        middle = (first + last) // 2
        return lax.cond(
            i < middle, lambda: run_cut(i, first, middle), lambda: run_cut(i, middle, last)
        )

    starts = next(i for i, op in enumerate(cuts[0]) if op[0] != "send")
    run(cuts[0][:starts])
    cuts[0] = cuts[0][starts:]
    spread(slab_one, full_one, 0)
    spread(slab_two, full_two, 1)

    @pl.loop(0, len(cuts))
    def _(i):
        rows = run_cut(i, 0, len(cuts))
        products_of(i // (len(cuts) // 2), rows)

    await_send(own_raw.at[pl.ds(0, (NX * NC - 1) * slab), :], swap_send)
    await_send(ring_z, sum_send.at[0])
    await_send(ring_y, sum_send.at[1])
    await_send(ring_z, sum_send.at[2])
    await_send(full_one.at[pl.ds(0, n_blocks - 1)], x_send.at[0])
    await_send(full_two.at[pl.ds(0, n_blocks - 1)], x_send.at[1])
    await_send(full_two.at[pl.ds(0, n_blocks - 1), pl.ds(0, 256), :], x_send.at[2])
    await_send(tiles.at[0, pl.ds(0, NY * NZ - 1)], tile_send.at[0])
    await_send(tiles.at[1, pl.ds(0, NY * NZ - 1)], tile_send.at[1])


GROUP = 16


def finish_kernel(
    rows_in, cols_in, lower_one, lower_two, upper, lower, partial, out_one, out_two, trailing, staged, rows, cols, sem
):
    index = [pltpu.make_async_copy(rows_in, rows, sem.at[2]), pltpu.make_async_copy(cols_in, cols, sem.at[3])]
    for copy in index:
        copy.start()
    n_slots = partial.shape[0]
    n_blocks = lower_one.shape[1] // partial.shape[-1]
    copies = [
        pltpu.make_async_copy(lower_one, out_one, sem.at[0]),
        pltpu.make_async_copy(lower_two, out_two, sem.at[1]),
    ]
    for copy in copies:
        copy.start()
    for copy in index:
        copy.wait()
    for g in range(n_slots // GROUP):

        @pl.loop(g * GROUP, (g + 1) * GROUP, unroll=4)
        def _(s):
            index = (cols[s] // n_blocks) * n_blocks + rows[s] % n_blocks
            staged[s, :64] = (partial[s, :64] - upper[index]).astype(staged.dtype)
            staged[s, 64:] = (partial[s, 64:] - lower[index]).astype(staged.dtype)

        part = pl.ds(g * GROUP, GROUP)
        copies.append(pltpu.make_async_copy(staged.at[part], trailing.at[part], sem.at[4 + g]))
        copies[-1].start()
    for copy in copies:
        copy.wait()


def per_device(
    panel_one,
    panel_two,
    inverse_one,
    inverse_two,
    column_blocks,
    row_map,
    targets,
    rows_one,
    cols_one,
    rows_two,
    cols_two,
):
    slab, row_count = panel_one.shape
    width = inverse_one.shape[0]
    size = targets.shape[-1]
    n_slots = targets.shape[2]
    n_blocks = row_count // size
    n_rows = NY * NZ
    bf16, f32 = jnp.bfloat16, jnp.float32
    vmem = pltpu.VMEM
    dma = pltpu.SemaphoreType.DMA
    in_hbm = pl.BlockSpec(memory_space=pltpu.HBM)
    smem = pltpu.SMEM
    in_vmem = pl.BlockSpec(memory_space=vmem)

    def stay(*arrays):
        return [pltpu.with_memory_space_constraint(array, pltpu.HBM) for array in arrays]

    held = pl.pallas_call(
        kernel,
        out_shape=(
            vmem(panel_one.shape, bf16),
            vmem(panel_two.shape, bf16),
            vmem((n_rows * n_blocks, size // 2, size), f32),
            vmem((n_rows * n_blocks, size // 2, size), f32),
            vmem((n_slots, size, size), f32),
        ),
        in_specs=[in_hbm] * 9,
        out_specs=(in_vmem,) * 5,
        scratch_shapes=[
            vmem((n_blocks, slab, size), bf16),
            vmem((n_blocks, slab, size), bf16),
            vmem((n_blocks, width, size), bf16),
            vmem((n_blocks, width, size), bf16),
            vmem((width, width), bf16),
            vmem((width, width), bf16),
            vmem((width, size), bf16),
            vmem((8, 32, size), bf16),
            vmem((NZ - 1, 32, size), bf16),
            vmem((32, size), bf16),
            vmem((NY - 1, 32, size), bf16),
            vmem((4, width, size), bf16),
            vmem((width, width), bf16),
            vmem((n_blocks, width, size), bf16),
            vmem((n_blocks, width, size), bf16),
            vmem((2, row_count, width), bf16),
            vmem((2, n_rows, width, size), bf16),
            vmem((n_slots, size, size), bf16),
            smem((4,), jnp.int32),
            smem((n_blocks,), jnp.int32),
            smem((n_slots,), jnp.int32),
            smem((n_slots,), jnp.int32),
            dma((8,)),
            dma((4,)),
            dma((3,)),
            dma((3, NX)),
            dma((3,)),
            dma,
            dma,
            dma((3,)),
            dma((3,)),
            dma((2,)),
            dma((2, N_EVENTS)),
        ],
        compiler_params=pltpu.CompilerParams(
            collective_id=0, has_side_effects=True, vmem_limit_bytes=VMEM_LIMIT
        ),
    )(
        *stay(
            panel_one,
            panel_two,
            inverse_one,
            inverse_two,
            targets.reshape(n_slots, size, size),
            column_blocks,
            row_map,
            rows_one.reshape(-1),
            cols_one.reshape(-1),
        )
    )
    lower_one, lower_two, trailing = pl.pallas_call(
        finish_kernel,
        out_shape=(
            jax.ShapeDtypeStruct(panel_one.shape, bf16),
            jax.ShapeDtypeStruct(panel_two.shape, bf16),
            jax.ShapeDtypeStruct((n_slots, size, size), bf16),
        ),
        in_specs=[in_hbm] * 2 + [in_vmem] * 5,
        out_specs=(in_hbm,) * 3,
        scratch_shapes=[
            vmem((n_slots, size, size), bf16),
            smem((n_slots,), jnp.int32),
            smem((n_slots,), jnp.int32),
            dma((4 + n_slots // GROUP,)),
        ],
        compiler_params=pltpu.CompilerParams(vmem_limit_bytes=FINISH_LIMIT),
    )(*stay(rows_two.reshape(-1), cols_two.reshape(-1)), *held)
    return lower_one, lower_two, trailing.reshape(targets.shape)


def solution(mesh):
    return jax.shard_map(
        per_device,
        mesh=mesh,
        in_specs=(
            P("col", "row"),
            P("col", "row"),
            P(),
            P(),
            P(),
            P("row"),
            P("row", "col", None, None, None),
            P("row", "col", None),
            P("row", "col", None),
            P("row", "col", None),
            P("row", "col", None),
        ),
        out_specs=(P("col", "row"), P("col", "row"), P("row", "col", None, None, None)),
        check_vma=False,
    )
```

```python
import functools
import heapq

import jax
import jax.numpy as jnp
from jax import lax
from jax.experimental import pallas as pl
from jax.experimental.pallas import tpu as pltpu
from jax.sharding import PartitionSpec as P

MESH = pl.DeviceIdType.MESH
NY, NZ, NX, NC = 4, 8, 4, 2

PART_A, HALF_A0, HALF_A1 = (0, 304), (0, 160), (160, 144)
PART_B, HALF_B0, HALF_B1 = (304, 208), (304, 112), (416, 96)
STEP = {"y+": (1, 0), "y-": (-1, 0), "z+": (0, 1), "z-": (0, -1)}
OWN_SENDS = (
    ("z+", PART_A),
    ("z-", PART_A),
    ("y+", PART_B),
    ("y-", PART_B),
    ("y+", PART_A),
    ("y-", PART_A),
    ("z+", PART_B),
    ("z-", PART_B),
)


def wrapped(value, size):
    value %= size
    return value - size if value > size // 2 else value


def next_source(source, way):
    dy, dz = STEP[way]
    return (wrapped(source[0] - dy, NY), wrapped(source[1] - dz, NZ))


def forwards(way, piece, source, seen):
    sy, sz = source
    if piece[0] < PART_A[1]:
        first, second = HALF_A0, HALF_A1
        if way[0] == "z":
            half = first if way == "z+" else second
            out = [(way, PART_A)] if abs(sz) < 3 else []
            if abs(sz) == 3:
                out.append((way, half))
            if abs(sz) < 4 or {first, second} <= seen:
                out += [("y+", PART_A), ("y-", PART_A)]
            return out
        return [(way, first if way == "y+" else second)] if abs(sy) == 1 else []
    first, second = HALF_B0, HALF_B1
    if way[0] == "y":
        out = []
        if abs(sy) == 1:
            out.append((way, first if way == "y+" else second))
        if abs(sy) == 1 or {first, second} <= seen:
            out += [("z+", PART_B), ("z-", PART_B)]
        return out
    if abs(sz) < 3:
        return [(way, PART_B)]
    return [(way, first if way == "z+" else second)] if abs(sz) == 3 else []


LINK_RATE, LATENCY, BACKLOG, PANEL_WEIGHT = 47.0, 2.8, 0.5, 0.5
SPREAD, MIX = 1.5, 41


def hops_left(way, piece, source):
    sy, sz = next_source(source, way)
    if piece[0] < PART_A[1]:
        return 2 - abs(sy) if way[0] == "y" else 4 - abs(sz) + 2
    return 4 - abs(sz) if way[0] == "z" else 2 - abs(sy) + 4


def receives():
    found, heap = [], [(w, p, next_source((0, 0), w)) for w, p in OWN_SENDS]
    seen = {}
    while heap:
        way, piece, source = heap.pop(0)
        found.append((way, piece, source))
        seen.setdefault(source, set()).add(piece)
        for onward, part in forwards(way, piece, source, seen[source]):
            heap.append((onward, part, next_source(source, onward)))
    return found


EVENTS = receives()
EVENT = {event: i for i, event in enumerate(EVENTS)}
N_EVENTS = len(EVENTS)
VMEM_LIMIT = 34 * 1024 * 1024
FINISH_LIMIT = 6 * 1024 * 1024
CHAIN = (
    ("sum_back", None, 4.4, 0.15),
    ("bridge_spread", "sum_back", 5.4, 0.05),
    ("one_1", None, 6.5, 0.02),
    ("one_3", None, 6.5, 0.02),
    ("one_2", None, 10.7, 0.02),
    ("one_side", "one_2", 2.4, 0.02),
    ("two_1", None, 9.5, 0.02),
    ("two_3", None, 9.5, 0.02),
    ("two_2", None, 13.0, 0.02),
    ("two_side", "two_2", 2.4, 0.02),
    ("bridge_1", "bridge_spread", 3.9, 0.02),
    ("bridge_3", "bridge_spread", 3.9, 0.02),
    ("bridge_2", "bridge_3", 2.9, 0.02),
    ("bridge_side", "bridge_2", 1.6, 0.02),
)


def make_program():
    free = dict.fromkeys(STEP, 0.0)
    arriving, pending, seen, rows = [], {way: [] for way in STEP}, ({}, {}), ({}, {})
    ready = ([(0, 0)], [])
    program, ended, state = [], {}, {"now": 0.0, "count": 0, "products": [0, 0], "combined": 0}
    chain = list(CHAIN)

    def queue(p, way, piece, source):
        state["count"] += 1
        vary = SPREAD * (state["count"] * MIX % 97) / 97
        rank = (PANEL_WEIGHT * p - hops_left(way, piece, source) + vary, state["count"])
        heapq.heappush(pending[way], (rank, p, piece, source))

    def ship(way):
        _, p, piece, source = heapq.heappop(pending[way])
        free[way] = max(free[way], state["now"]) + piece[1] * 256 / 1000 / LINK_RATE
        heapq.heappush(arriving, (free[way] + LATENCY, state["count"], p, way, piece, next_source(source, way)))
        state["count"] += 1
        program.append(("send", p, way, piece, source))
        state["now"] += 0.02

    def receive():
        _, _, p, way, piece, source = heapq.heappop(arriving)
        program.append(("wait", p, way, piece, source))
        state["now"] += 0.02
        seen[p].setdefault(source, set()).add(piece)
        rows[p][source] = rows[p].get(source, 0) + piece[1]
        for onward, part in forwards(way, piece, source, seen[p][source]):
            queue(p, onward, part, source)
        if rows[p][source] == 512:
            ready[p].append(source)

    steps = [("factor_one", i, 0.53, "one_side") for i in range(4)]
    steps += [("bridge_build", i, 0.55, "bridge_side") for i in range(2)]
    steps += [("factor_two", i, 0.86, "two_side") for i in range(4)]
    jobs = {name: [s for s in steps if s[0] == name] for name in ("factor_one", "bridge_build", "factor_two")}

    def job():
        for name, before in (("bridge_build", ()), ("factor_two", ("factor_one", "bridge_build")), ("factor_one", ())):
            if jobs[name] and not any(jobs[b] for b in before) and jobs[name][0][3] in ended:
                if ended[jobs[name][0][3]] <= state["now"] and (name != "factor_two" or "two_side" in ended):
                    _, i, cost, _ = jobs[name].pop(0)
                    return (name, i), cost
        free_to_run = (not jobs["factor_one"], state["combined"] == 8 and not jobs["factor_two"])
        for p in range(2):
            if free_to_run[p] and len(ready[p]) >= 2:
                return ("products", p) + (ready[p].pop(0), ready[p].pop(0)), 0.48
            if p == 0 and state["products"][0] == 32 and state["combined"] < 8:
                state["combined"] += 1
                return ("combine", state["combined"] - 1), 0.2
        return None, 0.0

    def begin(p):
        for way, piece in OWN_SENDS:
            queue(p, way, piece, (0, 0))

    begin(0)
    while True:
        now = state["now"]
        if arriving and arriving[0][0] <= now:
            receive()
            continue
        ways = [w for w in STEP if pending[w] and free[w] - now < BACKLOG]
        if ways:
            ship(min(ways, key=lambda w: free[w]))
            continue
        due = [c for c in chain if (c[1] is None or c[1] in ended) and (ended.get(c[1], 0.0) + c[2] <= now)]
        if due:
            chain.remove(due[0])
            program.append(("chain", due[0][0]))
            state["now"] += due[0][3]
            ended[due[0][0]] = state["now"]
            continue
        work, cost = job()
        if work:
            program.append(("job",) + work)
            state["now"] += cost
            if work[0] == "products":
                state["products"][work[1]] += len(work) - 2
            if work == ("factor_two", 0):
                ready[1].append((0, 0))
                begin(1)
            continue
        later = [arriving[0][0]] if arriving else []
        later += [free[w] - BACKLOG for w in STEP if pending[w]]
        later += [ended.get(c[1], 0.0) + c[2] for c in chain if c[1] is None or c[1] in ended]
        if not later:
            break
        state["now"] = max(now + 0.01, min(later))
    return program, state["now"]


PROGRAM, PLANNED = make_program()


def kernel(
    panel_one,
    panel_two,
    inverse_one,
    inverse_two,
    targets,
    column_blocks,
    row_map,
    rows_one,
    cols_one,
    lower_one,
    lower_two,
    upper,
    lower,
    partial,
    slab_one,
    slab_two,
    full_one,
    full_two,
    inv_one,
    inv_two,
    own_raw,
    pick,
    ring_z,
    mid,
    ring_y,
    raw_bridge,
    bridge_t,
    blocks_one,
    blocks_two,
    left,
    tiles,
    staged,
    bridge_from,
    map_from,
    pick_rows,
    pick_cols,
    local_sem,
    index_sem,
    x_send,
    x_recv,
    side_recv,
    swap_send,
    swap_recv,
    sum_send,
    sum_recv,
    tile_send,
    tile_recv,
):
    f32, bf16 = jnp.float32, jnp.bfloat16
    row, col = lax.axis_index("row"), lax.axis_index("col")
    y, z = row // NZ, row % NZ
    x, core = col // NC, col % NC
    slab = slab_one.shape[1]
    base = pl.multiple_of(col * slab, slab)

    def row_at(dy, dz):
        return ((y + dy + NY) % NY) * NZ + (z + dz + NZ) % NZ

    def col_at(dx):
        return ((x + dx) % NX) * NC + core

    partner = x * NC + (1 - core)

    def remote(src, dst, send, recv, device):
        return pltpu.make_async_remote_copy(
            src_ref=src, dst_ref=dst, send_sem=send, recv_sem=recv, device_id=device, device_id_type=MESH
        )

    def await_recv(ref, sem):
        remote(ref, ref, tile_send.at[0], sem, (row, partner)).wait_recv()

    def await_send(ref, sem):
        remote(ref, ref, sem, tile_recv.at[0, 0], (row, partner)).wait_send()

    barrier = pltpu.get_barrier_semaphore()
    in_row = [(row, (col + d) % (NX * NC)) for d in range(1, NX * NC)]
    along_z = [(row_at(0, d), col) for d in range(1, NZ)]
    along_y = [(row_at(d, 0), col) for d in range(1, NY)]
    for device in in_row + along_z + along_y:
        pl.semaphore_signal(barrier, inc=1, device_id=device, device_id_type=MESH)

    loads = []
    n_blocks = slab_one.shape[0]
    for which, (panel, mine) in enumerate(((panel_one, slab_one), (panel_two, slab_two))):
        for j in range(n_blocks):
            loads.append(pltpu.make_async_copy(panel.at[:, pl.ds(j * 128, 128)], mine.at[j], local_sem.at[which]))
    for copy in loads:
        copy.start()
    load_inv_one = pltpu.make_async_copy(inverse_one, inv_one, local_sem.at[2])
    load_inv_two = pltpu.make_async_copy(inverse_two, inv_two, local_sem.at[3])
    load_targets = pltpu.make_async_copy(targets, staged, local_sem.at[4])
    small = [(column_blocks, bridge_from), (row_map, map_from), (rows_one, pick_rows), (cols_one, pick_cols)]
    small = [pltpu.make_async_copy(src, dst, index_sem.at[i]) for i, (src, dst) in enumerate(small)]
    for copy in small:
        copy.start()
    load_inv_one.start()
    load_inv_two.start()
    load_targets.start()

    for copy in small:
        copy.wait()
    pltpu.make_async_copy(slab_one, slab_one, local_sem.at[0]).wait()
    pltpu.make_async_copy(slab_two, slab_two, local_sem.at[1]).wait()
    keep_one = pltpu.make_async_copy(slab_one, full_one.at[:, pl.ds(base, slab), :], local_sem.at[5])
    keep_two = pltpu.make_async_copy(slab_two, full_two.at[:, pl.ds(base, slab), :], local_sem.at[6])
    keep_raw = pltpu.make_async_copy(slab_one.at[col], own_raw.at[pl.ds(base, slab), :], local_sem.at[7])
    keep_one.start()
    keep_two.start()
    keep_raw.start()
    pl.semaphore_wait(barrier, len(in_row) + len(along_z) + len(along_y))

    for _, peer in in_row:
        remote(
            slab_one.at[peer], own_raw.at[pl.ds(base, slab), :], swap_send, swap_recv, (row, peer)
        ).start()

    for k in range(4):
        chosen = bridge_from[k]
        block = slab_one[chosen % n_blocks]
        block = jnp.where(chosen // n_blocks == row, block.astype(f32), 0.0).astype(bf16)
        pick[2 * k] = block[:32]
        pick[2 * k + 1] = block[32:]

    def slab_of(full, dx):
        return full.at[:, pl.ds(pl.multiple_of(col_at(NX - dx) * slab, slab), slab), :]

    def spread(mine, full, which):
        place = full.at[:, pl.ds(base, slab), :]
        for dx in (1, 3):
            remote(mine, place, x_send.at[which], x_recv.at[which, dx - 1], (row, col_at(dx))).start()
        remote(mine, place, x_send.at[which], side_recv.at[which], (row, partner)).start()

    def pass_on(full, which, dx):
        ref = slab_of(full, dx)
        half = full.shape[0] // 2
        if dx == 2:
            await_recv(ref.at[pl.ds(0, half)], x_recv.at[which, 1])
            await_recv(ref.at[pl.ds(half, half)], x_recv.at[which, 3])
        else:
            await_recv(ref, x_recv.at[which, dx - 1])
            part = ref.at[pl.ds(0 if dx == 1 else half, half)]
            remote(
                part, part, x_send.at[which], x_recv.at[which, 1 if dx == 1 else 3], (row, col_at(dx))
            ).start()
        remote(ref, ref, x_send.at[which], side_recv.at[which], (row, partner)).start()

    def side_wait(full, which):
        await_recv(full.at[:, pl.ds(0, NX * slab), :], side_recv.at[which])

    def sum_z_send():
        for d in range(1, NZ):
            remote(
                pick.at[(z + d) % NZ], ring_z.at[d - 1], sum_send.at[0], sum_recv.at[0], (row_at(0, d), col)
            ).start()

    piece_k = z // 2
    piece_rows = pl.ds(pl.multiple_of(base + 32 * (z % 2), 32), 32)

    def sum_y_send():
        await_recv(ring_z, sum_recv.at[0])
        total = pick[z].astype(f32)
        for d in range(NZ - 1):
            total += ring_z[d].astype(f32)
        mid[...] = total.astype(bf16)
        for d in range(1, NY):
            remote(mid, ring_y.at[d - 1], sum_send.at[1], sum_recv.at[1], (row_at(d, 0), col)).start()

    def sum_z_return():
        await_recv(ring_y, sum_recv.at[1])
        total = mid[...].astype(f32)
        for d in range(NY - 1):
            total += ring_y[d].astype(f32)
        raw_bridge[piece_k, piece_rows, :] = total.astype(bf16)
        ref = raw_bridge.at[piece_k, piece_rows, :]
        for d in range(1, NZ):
            remote(ref, ref, sum_send.at[2], sum_recv.at[2], (row_at(0, d), col)).start()

    def bridge_spread():
        await_recv(ring_z, sum_recv.at[2])
        spread(raw_bridge.at[:, pl.ds(base, slab), :], raw_bridge, 2)

    def tile_copy(p, way, piece, source):
        ref = tiles.at[p, row_at(*source), pl.ds(*piece), :]
        event = EVENT[(way, piece, next_source(source, way))]
        remote(ref, ref, tile_send.at[p], tile_recv.at[p, event], (row_at(*STEP[way]), col)).start()

    def tile_wait(p, way, piece, source):
        ref = tiles.at[p, row_at(*source), pl.ds(*piece), :]
        await_recv(ref, tile_recv.at[p, EVENT[(way, piece, source)]])

    def dot(a, b):
        return jnp.dot(a, b, preferred_element_type=f32)

    def first_block():
        await_recv(own_raw.at[pl.ds(0, (NX * NC - 1) * slab), :], swap_recv)
        tiles[0, row] = dot(inv_one[...], own_raw[...]).astype(bf16)

    def store_pair(blocks, p, i, value):
        for h in range(2):
            part = value[:, h * 128 : (h + 1) * 128]
            blocks[2 * i + h] = part.astype(bf16)
            left[p, pl.ds(pl.multiple_of((2 * i + h) * 128, 128), 128), :] = part.T.astype(bf16)

    def factor_one(i):
        pair = jnp.concatenate([full_one[2 * i], full_one[2 * i + 1]], axis=1)
        store_pair(blocks_one, 0, i, dot(inv_one[...], pair))
        if i == n_blocks // 2 - 1:
            write_lower(blocks_one, lower_one)

    def bridge_build(i):
        pair = jnp.concatenate([raw_bridge[2 * i], raw_bridge[2 * i + 1]], axis=1)
        bridge_t[i * 256 : (i + 1) * 256, :] = dot(inv_one[...], pair).T.astype(bf16)

    def pair_two(i):
        mapped = jnp.concatenate(
            [blocks_one[map_from[2 * i] % n_blocks], blocks_one[map_from[2 * i + 1] % n_blocks]], axis=1
        )
        pair = jnp.concatenate([full_two[2 * i], full_two[2 * i + 1]], axis=1)
        updated = (pair.astype(f32) - dot(bridge_t[...], mapped)).astype(bf16)
        store_pair(blocks_two, 1, i, dot(inv_two[...], updated))

    def factor_two(i):
        pair_two((col // 2 + i) % (n_blocks // 2))
        if i == 0:
            tiles[1, row] = blocks_two[col]
        if i == n_blocks // 2 - 1:
            write_lower(blocks_two, lower_two)

    def products_of(p, rows):
        value = dot(left[p], jnp.concatenate([tiles[p, t] for t in rows], axis=1))
        for h, t in enumerate(rows):
            part = value[:, h * 128 : (h + 1) * 128].reshape(n_blocks, 128, 128)
            upper[pl.ds(t * n_blocks, n_blocks)] = part[:, :64]
            lower[pl.ds(t * n_blocks, n_blocks)] = part[:, 64:]

    n_slots = staged.shape[0]

    def combine(g):
        if g == 0:
            load_targets.wait()

        @pl.loop(g * n_slots // 8, (g + 1) * n_slots // 8, unroll=4)
        def _(s):
            index = (pick_cols[s] // n_blocks) * n_blocks + pick_rows[s] % n_blocks
            partial[s, :64] = staged[s, :64].astype(f32) - upper[index]
            partial[s, 64:] = staged[s, 64:].astype(f32) - lower[index]

    def write_lower(blocks, out):
        for j in range(n_blocks):
            out[:, j * 128 : (j + 1) * 128] = blocks[j, pl.ds(base, slab), :]

    chain = {
        "sum_back": sum_z_return,
        "bridge_spread": bridge_spread,
        "one_side": lambda: side_wait(full_one, 0),
        "two_side": lambda: side_wait(full_two, 1),
        "bridge_side": lambda: side_wait(raw_bridge, 2),
    }
    for which, (name, full) in enumerate((("one", full_one), ("two", full_two), ("bridge", raw_bridge))):
        for dx in range(1, NX):
            chain[f"{name}_{dx}"] = functools.partial(pass_on, full, which, dx)
    jobs = {
        "factor_one": factor_one,
        "bridge_build": bridge_build,
        "factor_two": factor_two,
        "combine": combine,
    }

    sum_z_send()
    load_inv_one.wait()
    load_inv_two.wait()
    keep_raw.wait()
    keep_one.wait()
    keep_two.wait()
    first_block()
    sum_y_send()
    cuts, chosen = [[]], []
    for op in PROGRAM:
        if op[:2] == ("job", "products"):
            chosen.append(op[3:])
            cuts.append([])
        else:
            cuts[-1].append(op)
    cuts.pop()

    def run(ops):
        for kind, *what in ops:
            if kind == "send":
                tile_copy(*what)
            elif kind == "wait":
                tile_wait(*what)
            elif kind == "chain":
                chain[what[0]]()
            else:
                jobs[what[0]](*what[1:])

    def run_cut(i, first, last):
        if last - first == 1:
            run(cuts[first])
            return tuple(row_at(*source) for source in chosen[first])
        middle = (first + last) // 2
        return lax.cond(
            i < middle, lambda: run_cut(i, first, middle), lambda: run_cut(i, middle, last)
        )

    starts = next(i for i, op in enumerate(cuts[0]) if op[0] != "send")
    run(cuts[0][:starts])
    cuts[0] = cuts[0][starts:]
    spread(slab_one, full_one, 0)
    spread(slab_two, full_two, 1)

    @pl.loop(0, len(cuts))
    def _(i):
        rows = run_cut(i, 0, len(cuts))
        products_of(i // (len(cuts) // 2), rows)

    await_send(own_raw.at[pl.ds(0, (NX * NC - 1) * slab), :], swap_send)
    await_send(ring_z, sum_send.at[0])
    await_send(ring_y, sum_send.at[1])
    await_send(ring_z, sum_send.at[2])
    await_send(full_one.at[pl.ds(0, n_blocks - 1)], x_send.at[0])
    await_send(full_two.at[pl.ds(0, n_blocks - 1)], x_send.at[1])
    await_send(full_two.at[pl.ds(0, n_blocks - 1), pl.ds(0, 256), :], x_send.at[2])
    await_send(tiles.at[0, pl.ds(0, NY * NZ - 1)], tile_send.at[0])
    await_send(tiles.at[1, pl.ds(0, NY * NZ - 1)], tile_send.at[1])


GROUP = 16


def finish_kernel(
    rows_in, cols_in, lower_one, lower_two, upper, lower, partial, out_one, out_two, trailing, staged, rows, cols, sem
):
    index = [pltpu.make_async_copy(rows_in, rows, sem.at[2]), pltpu.make_async_copy(cols_in, cols, sem.at[3])]
    for copy in index:
        copy.start()
    n_slots = partial.shape[0]
    n_blocks = lower_one.shape[1] // partial.shape[-1]
    copies = [
        pltpu.make_async_copy(lower_one, out_one, sem.at[0]),
        pltpu.make_async_copy(lower_two, out_two, sem.at[1]),
    ]
    for copy in copies:
        copy.start()
    for copy in index:
        copy.wait()
    for g in range(n_slots // GROUP):

        @pl.loop(g * GROUP, (g + 1) * GROUP, unroll=4)
        def _(s):
            index = (cols[s] // n_blocks) * n_blocks + rows[s] % n_blocks
            staged[s, :64] = (partial[s, :64] - upper[index]).astype(staged.dtype)
            staged[s, 64:] = (partial[s, 64:] - lower[index]).astype(staged.dtype)

        part = pl.ds(g * GROUP, GROUP)
        copies.append(pltpu.make_async_copy(staged.at[part], trailing.at[part], sem.at[4 + g]))
        copies[-1].start()
    for copy in copies:
        copy.wait()


def per_device(
    panel_one,
    panel_two,
    inverse_one,
    inverse_two,
    column_blocks,
    row_map,
    targets,
    rows_one,
    cols_one,
    rows_two,
    cols_two,
):
    slab, row_count = panel_one.shape
    width = inverse_one.shape[0]
    size = targets.shape[-1]
    n_slots = targets.shape[2]
    n_blocks = row_count // size
    n_rows = NY * NZ
    bf16, f32 = jnp.bfloat16, jnp.float32
    vmem = pltpu.VMEM
    dma = pltpu.SemaphoreType.DMA
    in_hbm = pl.BlockSpec(memory_space=pltpu.HBM)
    smem = pltpu.SMEM
    in_vmem = pl.BlockSpec(memory_space=vmem)

    def stay(*arrays):
        return [pltpu.with_memory_space_constraint(array, pltpu.HBM) for array in arrays]

    held = pl.pallas_call(
        kernel,
        out_shape=(
            vmem(panel_one.shape, bf16),
            vmem(panel_two.shape, bf16),
            vmem((n_rows * n_blocks, size // 2, size), f32),
            vmem((n_rows * n_blocks, size // 2, size), f32),
            vmem((n_slots, size, size), f32),
        ),
        in_specs=[in_hbm] * 9,
        out_specs=(in_vmem,) * 5,
        scratch_shapes=[
            vmem((n_blocks, slab, size), bf16),
            vmem((n_blocks, slab, size), bf16),
            vmem((n_blocks, width, size), bf16),
            vmem((n_blocks, width, size), bf16),
            vmem((width, width), bf16),
            vmem((width, width), bf16),
            vmem((width, size), bf16),
            vmem((8, 32, size), bf16),
            vmem((NZ - 1, 32, size), bf16),
            vmem((32, size), bf16),
            vmem((NY - 1, 32, size), bf16),
            vmem((4, width, size), bf16),
            vmem((width, width), bf16),
            vmem((n_blocks, width, size), bf16),
            vmem((n_blocks, width, size), bf16),
            vmem((2, row_count, width), bf16),
            vmem((2, n_rows, width, size), bf16),
            vmem((n_slots, size, size), bf16),
            smem((4,), jnp.int32),
            smem((n_blocks,), jnp.int32),
            smem((n_slots,), jnp.int32),
            smem((n_slots,), jnp.int32),
            dma((8,)),
            dma((4,)),
            dma((3,)),
            dma((3, NX)),
            dma((3,)),
            dma,
            dma,
            dma((3,)),
            dma((3,)),
            dma((2,)),
            dma((2, N_EVENTS)),
        ],
        compiler_params=pltpu.CompilerParams(
            collective_id=0, has_side_effects=True, vmem_limit_bytes=VMEM_LIMIT
        ),
    )(
        *stay(
            panel_one,
            panel_two,
            inverse_one,
            inverse_two,
            targets.reshape(n_slots, size, size),
            column_blocks,
            row_map,
            rows_one.reshape(-1),
            cols_one.reshape(-1),
        )
    )
    lower_one, lower_two, trailing = pl.pallas_call(
        finish_kernel,
        out_shape=(
            jax.ShapeDtypeStruct(panel_one.shape, bf16),
            jax.ShapeDtypeStruct(panel_two.shape, bf16),
            jax.ShapeDtypeStruct((n_slots, size, size), bf16),
        ),
        in_specs=[in_hbm] * 2 + [in_vmem] * 5,
        out_specs=(in_hbm,) * 3,
        scratch_shapes=[
            vmem((n_slots, size, size), bf16),
            smem((n_slots,), jnp.int32),
            smem((n_slots,), jnp.int32),
            dma((4 + n_slots // GROUP,)),
        ],
        compiler_params=pltpu.CompilerParams(vmem_limit_bytes=FINISH_LIMIT),
    )(*stay(rows_two.reshape(-1), cols_two.reshape(-1)), *held)
    return lower_one, lower_two, trailing.reshape(targets.shape)


def solution(mesh):
    return jax.shard_map(
        per_device,
        mesh=mesh,
        in_specs=(
            P("col", "row"),
            P("col", "row"),
            P(),
            P(),
            P(),
            P("row"),
            P("row", "col", None, None, None),
            P("row", "col", None),
            P("row", "col", None),
            P("row", "col", None),
            P("row", "col", None),
        ),
        out_specs=(P("col", "row"), P("col", "row"), P("row", "col", None, None, None)),
        check_vma=False,
    )
```
